32 devices in a mesh: domain: 8 (over z, y), vec: 4 (over x, core).
Axes of the slice: x: 2, y: 2, z: 4, core: 2. Of those that a mesh axis runs over, the one named last changes fastest.
Arguments:
- vectors: float32 [4096, 512], P('domain', 'vec'), may hold values from -6 to 6
- hamiltonian: float32 [512, 128, 128], P('domain'), may hold values from -0.09375 to 0.09375
- tile_pairs: int32 [512, 2], P('domain'), may hold values from 0 to 31, as said below
- tile_counts: int32 [8], P('domain'), may hold values from 8 to 64, as said below
Outputs:
- filtered: float32 [4096, 512], P('domain', 'vec')
- gram: float32 [512, 512], P('vec')
The draws below stay inside these ranges and needn't reach their ends.
Inputs may be any that keep to these rules, and one draw needn't show every extreme that they name: `tile_pairs`: slots k * 64 to (k + 1) * 64 - 1 have their row group r among groups k * 4 to (k + 1) * 4 - 1 and their column group c with r <= c <= min(k * 4 + 3 * 4 - 1, 31); pairs may repeat, and repeated blocks add. `tile_counts`: one domain index uses all 64 slots.
All inputs are finite; a program needn't handle non-finite values.
Results may differ from the reference program's by a relative error of at most 0.0003.
Values sent between devices are 32-bit elements; how exact they have to be, the bound alone decides.
A program may use at most 64 MiB of HBM per device.

```python
import jax
import jax.numpy as jnp
from jax import lax

TILE = 128
COLS = 512
G_DEV = 4
TILE_DEV = 64
REACH = 2
NGROUPS = 32
SLOTS = 512
ROWS = 4096


def draw_tile_pairs(key, part):
    ndev = NGROUPS // G_DEV
    first_key, second_key = jax.random.split(jax.random.fold_in(key, 11))
    span = (REACH + 1) * G_DEV
    row_loc = jax.random.randint(first_key, (ndev, TILE_DEV), 0, G_DEV)
    offset = jax.random.randint(second_key, (ndev, TILE_DEV), 0, span)
    col_loc = row_loc + offset % (span - row_loc)
    slot = jnp.arange(TILE_DEV, dtype=jnp.int32)[None, :]
    row_loc = jnp.where(slot == 0, 0, row_loc)
    col_loc = jnp.where(slot == 0, span - 1, col_loc)
    base = jnp.arange(ndev, dtype=jnp.int32)[:, None] * G_DEV
    row_grp = base + row_loc
    col_grp = jnp.minimum(base + col_loc, NGROUPS - 1)
    return jnp.stack([row_grp, col_grp], -1).reshape(SLOTS, 2).astype(jnp.int32)


def draw_tile_counts(key, part):
    ndev = NGROUPS // G_DEV
    first_key, second_key = jax.random.split(jax.random.fold_in(key, 23))
    counts = jax.random.randint(first_key, (ndev,), TILE_DEV // 8, TILE_DEV // 2 + 1)
    busiest = jax.random.randint(second_key, (), 0, ndev)
    counts = jnp.where(jnp.arange(ndev, dtype=jnp.int32) == busiest, TILE_DEV, counts)
    return counts.astype(jnp.int32)


def levels(rng, dims, shards, least, top_value):
    loudness = 1.0
    for position, parts in shards:
        draws = jax.random.uniform(jax.random.fold_in(jax.random.fold_in(rng, 6), position), (parts,), jnp.float32, least / len(shards), top_value / len(shards))
        loudness = loudness * jnp.repeat(jnp.exp(draws), dims[position] // parts).reshape((-1,) + (1,) * (len(dims) - 1 - position))
    return loudness


def centred(own_key, dims, scale, reach, shards=(), kind=jnp.bfloat16):
    loudness = levels(own_key, dims, shards, -0.22, 0.18) if shards else 1.0
    values = jax.random.normal(own_key, dims, jnp.float32) * scale * loudness
    return jnp.minimum(jnp.maximum(values, -reach), reach).astype(kind)


def setup_inputs(seed: int = 0) -> dict:
    keys = jax.random.split(jax.random.key(seed), 5)
    return {
        "vectors": centred(keys[0], (ROWS, COLS), 1.0, 6.0, ((0, 8), (1, 4)), jnp.float32),
        "hamiltonian": centred(keys[1], (SLOTS, TILE, TILE), (2 * TILE * TILE_DEV // G_DEV) ** -0.5, 0.09375, ((0, 8),), jnp.float32),
        "tile_pairs": draw_tile_pairs(jax.random.fold_in(keys[4], 71), 0),
        "tile_counts": draw_tile_counts(jax.random.fold_in(keys[4], 71), 0),
    }


center_shift = 1.0
half_width = 1.5


def apply_ham(block, hamiltonian, tile_pairs, weights):
    grouped = block.reshape(NGROUPS, TILE, COLS)
    total_slots = hamiltonian.shape[0]
    tiles = hamiltonian.reshape(total_slots // 64, 64, TILE, TILE)
    rows = tile_pairs[:, 0].reshape(total_slots // 64, 64)
    cols = tile_pairs[:, 1].reshape(total_slots // 64, 64)
    wts = weights.reshape(total_slots // 64, 64)

    def one_block(acc, items):
        tile, row_ids, col_ids, wgt = items
        diag = row_ids == col_ids
        tile = jnp.where(diag[:, None, None], 0.5 * (tile + jnp.swapaxes(tile, 1, 2)), tile)
        fwd = jnp.einsum("tij,tjc->tic", tile, grouped[col_ids], precision=lax.Precision.HIGHEST)
        back = jnp.einsum("tji,tjc->tic", tile, grouped[row_ids], precision=lax.Precision.HIGHEST)
        fwd = fwd * wgt[:, None, None]
        back = back * (wgt * (1.0 - diag.astype(jnp.float32)))[:, None, None]
        acc = acc.at[row_ids].add(fwd)
        acc = acc.at[col_ids].add(back)
        return acc, None

    start = jnp.zeros((NGROUPS, TILE, COLS), jnp.float32)
    result, _ = lax.scan(one_block, start, (tiles, rows, cols, wts))
    return result.reshape(NGROUPS * TILE, COLS)


def reference(vectors, hamiltonian, tile_pairs, tile_counts):
    total_slots = hamiltonian.shape[0]
    slot_ids = jnp.arange(total_slots, dtype=jnp.int32)
    owners = slot_ids // TILE_DEV
    weights = (slot_ids % TILE_DEV < tile_counts[owners]).astype(jnp.float32)
    first = vectors
    second = (apply_ham(first, hamiltonian, tile_pairs, weights) - center_shift * first) / half_width
    third = 2.0 * (apply_ham(second, hamiltonian, tile_pairs, weights) - center_shift * second) / half_width - first
    filtered = 2.0 * (apply_ham(third, hamiltonian, tile_pairs, weights) - center_shift * third) / half_width - second
    gram = jnp.dot(filtered.T, filtered, precision=lax.Precision.HIGHEST, preferred_element_type=jnp.float32) / ROWS
    return filtered, gram
```

```python
import functools

import jax
import jax.numpy as jnp
from jax import lax
from jax.experimental import pallas as pl
from jax.experimental.pallas import tpu as pltpu
from jax.sharding import PartitionSpec as P

TILE = 128
REACH = 2

center_shift = 1.0
half_width = 1.5

F32 = jnp.float32
BF16 = jnp.bfloat16


def halves(value):
    high = value.astype(BF16)
    low = (value - high.astype(F32)).astype(BF16)
    return high, low


def stacked(value):
    return jnp.concatenate(halves(value), 1)


def left_lanes(value):
    return lax.broadcasted_iota(jnp.int32, value.shape, 1) < value.shape[1] // 2


def swapped(value):
    return pltpu.roll(value, value.shape[1] // 2, 1)


def packed(value):
    upper, lower = value[: value.shape[0] // 2], value[value.shape[0] // 2 :]
    left = left_lanes(upper)
    return jnp.where(left, upper, swapped(lower)), jnp.where(left, swapped(upper), lower)


def unpacked(first, second):
    left = left_lanes(first)
    return jnp.where(left, first, swapped(second)), jnp.where(left, swapped(first), second)


def product(high, low, both):
    wide = jnp.dot(high, both, preferred_element_type=F32)
    wide = wide + jnp.dot(low, both, preferred_element_type=F32)
    width = both.shape[1] // 2
    return wide[:, :width] + wide[:, width:]


def packed_product(high, low, both):
    wide = jnp.dot(high, both, preferred_element_type=F32)
    wide = wide + jnp.dot(low, both, preferred_element_type=F32)
    wide = wide + swapped(wide)
    half = wide.shape[0] // 2
    return jnp.where(left_lanes(wide[:half]), wide[:half], wide[half:])


def put_stacked(both, value):
    high = value.astype(BF16).astype(F32)
    low = value - high
    left = left_lanes(value)
    half = value.shape[0]
    both[:half] = jnp.where(left, high, swapped(low)).astype(BF16)
    both[half:] = jnp.where(left, swapped(high), low).astype(BF16)


def put_index(groups, me, pairs, count, index_ref):
    slots = pairs.shape[1]
    span = (REACH + 1) * groups
    lanes = index_ref.shape[1]
    code = (pairs[0:1] - me * groups) * span + pairs[1:2] - me * groups
    row = lax.broadcasted_iota(jnp.int32, (slots, slots), 0)
    lane = lax.broadcasted_iota(jnp.int32, (slots, slots), 1)
    down = jnp.sum(jnp.where(row == lane, code, 0), axis=1, keepdims=True)
    same = (down == code) & (row < lane) & (lane < count)
    index_ref[0:1, :slots] = jnp.max(jnp.where(same, row, -1), axis=0, keepdims=True)
    row = lax.broadcasted_iota(jnp.int32, (slots, lanes), 0)
    lane = lax.broadcasted_iota(jnp.int32, (slots, lanes), 1)
    here = (down == lane) & (row < count)
    index_ref[1:2] = jnp.max(jnp.where(here, row, -1), axis=0, keepdims=True)


def filter_kernel(n, m, with_gram, x_ref, pairs_ref, count_ref, ham_ref, *refs):
    if with_gram:
        f_ref, g_ref, *refs = refs
    else:
        f_ref, *refs = refs
    (tiles, x0, pairs, index_v, index_s, fwd_h, fwd_l, back_h, back_l, both, both_half) = refs[:11]
    (acc, xs, in_x0, in_x, in_b, out_b) = refs[11:17]
    (load_sem, x0s_sem, x0r_sem, xs_sem, xr_sem, bs_sem, br_sem) = refs[17:24]
    me = lax.axis_index("domain")
    mine = lax.axis_index("vec")
    rows, width = x_ref.shape
    half = rows // 2
    groups = rows // TILE
    span = (REACH + 1) * groups

    load_pairs = pltpu.make_async_copy(pairs_ref, pairs, load_sem.at[0])
    load_pairs.start()
    load_x = pltpu.make_async_copy(x_ref, x0, load_sem.at[1])
    load_x.start()
    load_tiles = pltpu.make_async_copy(ham_ref, tiles, load_sem.at[2])
    load_tiles.start()

    barrier = pltpu.get_barrier_semaphore()
    if with_gram:
        for d in range(1, n):
            pl.semaphore_signal(barrier, inc=1, device_id={"domain": (me + d) % n})
        for d in range(1, m):
            pl.semaphore_signal(barrier, inc=1, device_id={"vec": (mine + d) % m})
    else:
        for d in range(1, REACH + 1):

            @pl.when(me >= d)
            def _():
                pl.semaphore_signal(barrier, inc=1, device_id={"domain": me - d})

            @pl.when(me + d < n)
            def _():
                pl.semaphore_signal(barrier, inc=1, device_id={"domain": me + d})

    load_pairs.wait()
    put_index(groups, me, pairs[...], count_ref[0], index_v)
    load_index = pltpu.make_async_copy(index_v, index_s, load_sem.at[3])
    load_index.start()

    if with_gram:
        pl.semaphore_wait(barrier, n - 1 + m - 1)
    else:
        for d in range(1, REACH + 1):

            @pl.when(me >= d)
            def _():
                pl.semaphore_wait(barrier, 1)

            @pl.when(me + d < n)
            def _():
                pl.semaphore_wait(barrier, 1)

    def rows_at(group):
        return pl.ds(group * TILE, TILE)

    def x0_copy(d):
        return pltpu.make_async_remote_copy(
            src_ref=x0,
            dst_ref=in_x0.at[d - 1],
            send_sem=x0s_sem.at[d - 1],
            recv_sem=x0r_sem.at[d - 1],
            device_id={"domain": me - d},
        )

    def x_copy(step, part, d):
        return pltpu.make_async_remote_copy(
            src_ref=xs.at[step, part],
            dst_ref=in_x.at[step - 1, part, d - 1],
            send_sem=xs_sem.at[step - 1, part, d - 1],
            recv_sem=xr_sem.at[step - 1, part, d - 1],
            device_id={"domain": me - d},
        )

    def b_copy(step, part, d):
        return pltpu.make_async_remote_copy(
            src_ref=out_b.at[step, part, d - 1],
            dst_ref=in_b.at[step, part, d - 1],
            send_sem=bs_sem.at[step, part, d - 1],
            recv_sem=br_sem.at[step, part, d - 1],
            device_id={"domain": me + d},
        )

    if with_gram:
        (in_f, part, in_g1, out_g, in_g2, in_h, in_k) = refs[24:31]
        (fs_sem, fr_sem, g1s_sem, g1r_sem, g2s_sem, g2r_sem, hs_sem, hr_sem, ks_sem, kr_sem) = refs[31:]
        far = (mine + 2) % 4
        near = mine + 1 - 2 * (mine % 2)
        cross = (near + 2) % 4

        def f_copy(index, group):
            source = in_f.at[0] if index == 2 else f_ref
            return pltpu.make_async_remote_copy(
                src_ref=source.at[rows_at(group)],
                dst_ref=in_f.at[index, rows_at(group)],
                send_sem=fs_sem.at[index, group],
                recv_sem=fr_sem.at[index, group],
                device_id={"vec": far if index == 0 else near},
            )

    load_x.wait()
    for d in range(1, REACH + 1):

        @pl.when(me >= d)
        def _():
            x0_copy(d).start()

    both[...] = stacked(x0[...])
    xs[0, 0], xs[0, 1] = packed(x0[...])
    load_index.wait()
    load_tiles.wait()

    def add_before(slot, carry):
        before = index_s[0, slot]
        weight = (before >= 0).astype(F32)
        tiles[slot] = tiles[slot] + tiles[jnp.maximum(before, 0)] * weight
        return carry

    lax.fori_loop(0, tiles.shape[0], add_before, 0)

    def block_at(row, col):
        slot = index_s[1, row * span + col]
        return tiles[jnp.maximum(slot, 0)] * (slot >= 0).astype(F32)

    def put(high, low, index, row, col, value):
        high[index, rows_at(row), rows_at(col)], low[index, rows_at(row), rows_at(col)] = halves(value)

    for d in range(1, REACH + 1):
        for row in range(groups):
            for col in range(groups):
                block = block_at(row, d * groups + col)
                put(fwd_h, fwd_l, d, row, col, block)
                put(back_h, back_l, d - 1, col, row, block.T)

        @pl.when(me + d < n)
        def _():
            first, second = packed(product(back_h[d - 1], back_l[d - 1], both[...]))
            out_b[0, 0, d - 1] = first
            b_copy(0, 0, d).start()
            out_b[0, 1, d - 1] = second
            b_copy(0, 1, d).start()

    for row in range(groups):
        for col in range(row, groups):
            block = block_at(row, col)
            if row == col:
                put(fwd_h, fwd_l, 0, row, col, 0.5 * (block + block.T))
            else:
                put(fwd_h, fwd_l, 0, row, col, block)
                put(fwd_h, fwd_l, 0, col, row, block.T)

    acc[0], acc[1] = packed(product(fwd_h[0], fwd_l[0], both[...]))
    for d in range(1, REACH + 1):

        @pl.when(me + d < n)
        def _():
            x0_copy(d).wait_recv()
            first, second = packed(product(fwd_h[d], fwd_l[d], stacked(in_x0[d - 1])))
            acc[0] += first
            acc[1] += second

    def add_back(step, part):
        for d in range(1, REACH + 1):

            @pl.when(me >= d)
            def _():
                b_copy(step, part, d).wait_recv()
                acc[part] += in_b[step, part, d - 1]

    def start_step(step, part):
        for d in range(1, REACH + 1):

            @pl.when(me >= d)
            def _():
                x_copy(step, part, d).start()

        put_stacked(both_half, xs[step, part])
        for d in range(1, REACH + 1):

            @pl.when(me + d < n)
            def _():
                out_b[step, part, d - 1] = packed_product(back_h[d - 1], back_l[d - 1], both_half[...])
                b_copy(step, part, d).start()

        acc[part] = packed_product(fwd_h[0], fwd_l[0], both_half[...])

    def first_step(part, carry):
        add_back(0, part)
        xs[1, part] = (acc[part] - center_shift * xs[0, part]) / half_width
        start_step(1, part)
        return carry

    lax.fori_loop(0, 2, first_step, 0)

    def later_step(turn, carry):
        step, part = 1 + turn // 2, turn % 2
        for d in range(1, REACH + 1):

            @pl.when(me + d < n)
            def _():
                x_copy(step, part, d).wait_recv()
                put_stacked(both_half, in_x[step - 1, part, d - 1])
                acc[part] += packed_product(fwd_h[d], fwd_l[d], both_half[...])

        add_back(step, part)
        xs[step + 1, part] = 2.0 * (acc[part] - center_shift * xs[step, part]) / half_width - xs[step - 1, part]

        @pl.when(turn < 2)
        def _():
            start_step(step + 1, part)

        return carry

    lax.fori_loop(0, 4, later_step, 0)
    f_ref[:half], f_ref[half:] = unpacked(xs[3, 0], xs[3, 1])

    if with_gram:
        for group in range(groups):
            f_copy(0, group).start()
            f_copy(1, group).start()

    if with_gram:
        left_h, left_l = halves(f_ref[...].T)
        back_h[0, :width], back_l[0, :width] = left_h, left_l
        total = rows * n

        piece = width // n
        pairs = n // 2
        pair = me // 2
        side = me % 2
        mate = me + 1 - 2 * side
        owners = (mine, near, far, cross)

        def rows_of(owner):
            return pl.ds(pl.multiple_of(owner * piece, piece), piece)

        def at(column, owner):
            return (rows_of(owner), pl.ds(pl.multiple_of(owners[column] * width, width), width))

        def g1_copy(column, d):
            return pltpu.make_async_remote_copy(
                src_ref=part.at[column, rows_of(2 * ((pair + d) % pairs) + 1 - side)],
                dst_ref=in_g1.at[column, d],
                send_sem=g1s_sem.at[column, d],
                recv_sem=g1r_sem.at[column, d],
                device_id={"domain": mate},
            )

        def g2_copy(column, d):
            return pltpu.make_async_remote_copy(
                src_ref=out_g.at[column, d],
                dst_ref=in_g2.at[column, d],
                send_sem=g2s_sem.at[column, d],
                recv_sem=g2r_sem.at[column, d],
                device_id={"domain": 2 * ((pair + d) % pairs) + side},
            )

        def h_copy(column, d):
            return pltpu.make_async_remote_copy(
                src_ref=out_g.at[column, 0],
                dst_ref=in_h.at[column, d],
                send_sem=hs_sem.at[column, d],
                recv_sem=hr_sem.at[column, d],
                device_id={"domain": 2 * ((pair + d) % pairs) + side},
            )

        def k_copy(column, d):
            return pltpu.make_async_remote_copy(
                src_ref=out_g.at[column, 0] if d == 0 else in_h.at[column, d],
                dst_ref=in_k.at[column, d],
                send_sem=ks_sem.at[column, d],
                recv_sem=kr_sem.at[column, d],
                device_id={"domain": mate},
            )

        order = list(range(1, pairs)) + [0]

        def multiply(column, value):
            block = product(back_h[0, :width], back_l[0, :width], stacked(value)) / total
            part[column] = block
            for d in order:
                g1_copy(column, d).start()

        def add_mate(column):
            for d in order:
                g1_copy(column, d).wait_recv()
                out_g[column, d] = part[column, rows_of(2 * ((pair + d) % pairs) + side)] + in_g1[column, d]
                if d > 0:
                    g2_copy(column, d).start()

        def add_pairs(column):
            block = out_g[column, 0]
            for d in range(1, pairs):
                g2_copy(column, d).wait_recv()
                block = block + in_g2[column, d]
            out_g[column, 0] = block
            for d in range(1, pairs):
                h_copy(column, d).start()
            k_copy(column, 0).start()
            g_ref[at(column, me)] = block

        def from_pairs(column):
            for d in range(1, pairs):
                h_copy(column, d).wait_recv()
                k_copy(column, d).start()
                g_ref[at(column, 2 * ((pair + pairs - d) % pairs) + side)] = in_h[column, d]

        def from_mate(column):
            for d in range(pairs):
                k_copy(column, d).wait_recv()
                g_ref[at(column, 2 * ((pair + pairs - d) % pairs) + 1 - side)] = in_k[column, d]

        multiply(0, f_ref[...])
        for group in range(groups):
            f_copy(1, group).wait_recv()
        multiply(1, in_f[1])
        for group in range(groups):
            f_copy(0, group).wait_recv()
            f_copy(2, group).start()
        multiply(2, in_f[0])
        add_mate(0)
        add_mate(1)
        for group in range(groups):
            f_copy(2, group).wait_recv()
        multiply(3, in_f[2])
        add_mate(2)
        add_pairs(0)
        add_pairs(1)
        add_mate(3)
        add_pairs(2)
        from_pairs(0)
        from_pairs(1)
        add_pairs(3)
        from_pairs(2)
        from_mate(0)
        from_mate(1)
        from_pairs(3)
        from_mate(2)
        from_mate(3)
        for group in range(groups):
            for index in range(3):
                f_copy(index, group).wait_send()
        for column in range(4):
            for d in range(pairs):
                g1_copy(column, d).wait_send()
                k_copy(column, d).wait_send()
            for d in range(1, pairs):
                g2_copy(column, d).wait_send()
                h_copy(column, d).wait_send()

    for d in range(1, REACH + 1):

        @pl.when(me >= d)
        def _():
            x0_copy(d).wait_send()
            for step in range(1, 3):
                for part in range(2):
                    x_copy(step, part, d).wait_send()

        @pl.when(me + d < n)
        def _():
            for step in range(3):
                for part in range(2):
                    b_copy(step, part, d).wait_send()


def shards(vectors, hamiltonian, tile_pairs, tile_counts):
    n = lax.axis_size("domain")
    m = lax.axis_size("vec")
    rows, width = vectors.shape
    groups = rows // TILE
    half = rows // 2
    slots = tile_pairs.shape[0]
    lanes = -(-max(slots, (REACH + 1) * groups * groups) // 128) * 128
    with_gram = m == 4 and n % 2 == 0 and width % (8 * n) == 0
    dma = pltpu.SemaphoreType.DMA
    out_shape = [jax.ShapeDtypeStruct((rows, width), F32)]
    scratch = [
        pltpu.VMEM(hamiltonian.shape, F32),
        pltpu.VMEM((rows, width), F32),
        pltpu.VMEM((2, slots), jnp.int32),
        pltpu.VMEM((2, lanes), jnp.int32),
        pltpu.SMEM((2, lanes), jnp.int32),
        pltpu.VMEM((REACH + 1, rows, rows), BF16),
        pltpu.VMEM((REACH + 1, rows, rows), BF16),
        pltpu.VMEM((REACH, rows, rows), BF16),
        pltpu.VMEM((REACH, rows, rows), BF16),
        pltpu.VMEM((rows, 2 * width), BF16),
        pltpu.VMEM((rows, width), BF16),
        pltpu.VMEM((2, half, width), F32),
        pltpu.VMEM((4, 2, half, width), F32),
        pltpu.VMEM((REACH, rows, width), F32),
        pltpu.VMEM((2, 2, REACH, half, width), F32),
        pltpu.VMEM((3, 2, REACH, half, width), F32),
        pltpu.VMEM((3, 2, REACH, half, width), F32),
        dma((4,)),
        dma((REACH,)),
        dma((REACH,)),
        dma((2, 2, REACH)),
        dma((2, 2, REACH)),
        dma((3, 2, REACH)),
        dma((3, 2, REACH)),
    ]
    if with_gram:
        out_shape.append(jax.ShapeDtypeStruct((width, m * width), F32))
        scratch += [
            pltpu.VMEM((3, rows, width), F32),
            pltpu.VMEM((m, width, width), F32),
            dma((3, groups)),
            dma((3, groups)),
        ]
        scratch[-2:-2] = [pltpu.VMEM((m, n // 2, width // n, width), F32)] * 5
        scratch += [dma((m, n // 2))] * 8
    outs = pl.pallas_call(
        functools.partial(filter_kernel, n, m, with_gram),
        out_shape=out_shape,
        in_specs=[
            pl.BlockSpec(memory_space=pltpu.HBM),
            pl.BlockSpec(memory_space=pltpu.HBM),
            pl.BlockSpec(memory_space=pltpu.SMEM),
            pl.BlockSpec(memory_space=pltpu.HBM),
        ],
        out_specs=[pl.BlockSpec(memory_space=pltpu.VMEM)] * len(out_shape),
        scratch_shapes=scratch,
        compiler_params=pltpu.CompilerParams(
            collective_id=0, has_side_effects=True, vmem_limit_bytes=52 * 2**20
        ),
        name="chebyshev",
    )(vectors, tile_pairs.T, tile_counts, hamiltonian)
    if with_gram:
        return tuple(outs)
    (filtered,) = outs
    gathered = lax.all_gather(filtered, "vec", axis=1, tiled=True)
    partial_block = jnp.dot(
        filtered.T, gathered, precision=lax.Precision.HIGHEST, preferred_element_type=F32
    ) / (rows * n)
    return (filtered, lax.psum(partial_block, "domain"))


def solution(mesh):
    in_specs = (P("domain", "vec"), P("domain", None, None), P("domain", None), P("domain"))
    out_specs = (P("domain", "vec"), P("vec", None))
    return jax.shard_map(shards, mesh=mesh, in_specs=in_specs, out_specs=out_specs, check_vma=False)
```

```python
import functools

import jax
import jax.numpy as jnp
from jax import lax
from jax.experimental import pallas as pl
from jax.experimental.pallas import tpu as pltpu
from jax.sharding import PartitionSpec as P

TILE = 128
REACH = 2

center_shift = 1.0
half_width = 1.5

F32 = jnp.float32
BF16 = jnp.bfloat16


def halves(value):
    high = value.astype(BF16)
    low = (value - high.astype(F32)).astype(BF16)
    return high, low


def stacked(value):
    return jnp.concatenate(halves(value), 1)


def left_lanes(value):
    return lax.broadcasted_iota(jnp.int32, value.shape, 1) < value.shape[1] // 2


def swapped(value):
    return pltpu.roll(value, value.shape[1] // 2, 1)


def packed(value):
    upper, lower = value[: value.shape[0] // 2], value[value.shape[0] // 2 :]
    left = left_lanes(upper)
    return jnp.where(left, upper, swapped(lower)), jnp.where(left, swapped(upper), lower)


def unpacked(first, second):
    left = left_lanes(first)
    return jnp.where(left, first, swapped(second)), jnp.where(left, swapped(first), second)


def product(high, low, both):
    wide = jnp.dot(high, both, preferred_element_type=F32)
    wide = wide + jnp.dot(low, both, preferred_element_type=F32)
    width = both.shape[1] // 2
    return wide[:, :width] + wide[:, width:]


def packed_product(high, low, both):
    wide = jnp.dot(high, both, preferred_element_type=F32)
    wide = wide + jnp.dot(low, both, preferred_element_type=F32)
    wide = wide + swapped(wide)
    half = wide.shape[0] // 2
    return jnp.where(left_lanes(wide[:half]), wide[:half], wide[half:])


def put_stacked(both, at, value):
    high = value.astype(BF16).astype(F32)
    low = value - high
    left = left_lanes(value)
    half, width = value.shape
    columns = pl.ds(at * width, width)
    both[:half, columns] = jnp.where(left, high, swapped(low)).astype(BF16)
    both[half:, columns] = jnp.where(left, swapped(high), low).astype(BF16)


def put_index(groups, me, pairs, count, index_ref):
    slots = pairs.shape[1]
    span = (REACH + 1) * groups
    lanes = index_ref.shape[1]
    code = (pairs[0:1] - me * groups) * span + pairs[1:2] - me * groups
    row = lax.broadcasted_iota(jnp.int32, (slots, slots), 0)
    lane = lax.broadcasted_iota(jnp.int32, (slots, slots), 1)
    down = jnp.sum(jnp.where(row == lane, code, 0), axis=1, keepdims=True)
    same = (down == code) & (row < lane) & (lane < count)
    index_ref[0:1, :slots] = jnp.max(jnp.where(same, row, -1), axis=0, keepdims=True)
    row = lax.broadcasted_iota(jnp.int32, (slots, lanes), 0)
    lane = lax.broadcasted_iota(jnp.int32, (slots, lanes), 1)
    here = (down == lane) & (row < count)
    index_ref[1:2] = jnp.max(jnp.where(here, row, -1), axis=0, keepdims=True)


def filter_kernel(n, m, with_gram, x_ref, pairs_ref, count_ref, ham_ref, *refs):
    if with_gram:
        f_ref, g_ref, *refs = refs
    else:
        f_ref, *refs = refs
    (tiles, x0, pairs, index_v, index_s, fwd_h, fwd_l, back_h, back_l, both, both_half) = refs[:11]
    (acc, xs, in_x0, in_x, in_b, out_b) = refs[11:17]
    (load_sem, x0s_sem, x0r_sem, xs_sem, xr_sem, bs_sem, br_sem) = refs[17:24]
    me = lax.axis_index("domain")
    mine = lax.axis_index("vec")
    rows, width = x_ref.shape
    half = rows // 2
    groups = rows // TILE
    span = (REACH + 1) * groups

    load_pairs = pltpu.make_async_copy(pairs_ref, pairs, load_sem.at[0])
    load_pairs.start()
    load_x = pltpu.make_async_copy(x_ref, x0, load_sem.at[1])
    load_x.start()
    load_tiles = pltpu.make_async_copy(ham_ref, tiles, load_sem.at[2])
    load_tiles.start()

    barrier = pltpu.get_barrier_semaphore()
    if with_gram:
        for d in range(1, n):
            pl.semaphore_signal(barrier, inc=1, device_id={"domain": (me + d) % n})
        for d in range(1, m):
            pl.semaphore_signal(barrier, inc=1, device_id={"vec": (mine + d) % m})
    else:
        for d in range(1, REACH + 1):

            @pl.when(me >= d)
            def _():
                pl.semaphore_signal(barrier, inc=1, device_id={"domain": me - d})

            @pl.when(me + d < n)
            def _():
                pl.semaphore_signal(barrier, inc=1, device_id={"domain": me + d})

    load_pairs.wait()
    put_index(groups, me, pairs[...], count_ref[0], index_v)
    load_index = pltpu.make_async_copy(index_v, index_s, load_sem.at[3])
    load_index.start()

    if with_gram:
        pl.semaphore_wait(barrier, n - 1 + m - 1)
    else:
        for d in range(1, REACH + 1):

            @pl.when(me >= d)
            def _():
                pl.semaphore_wait(barrier, 1)

            @pl.when(me + d < n)
            def _():
                pl.semaphore_wait(barrier, 1)

    def rows_at(group):
        return pl.ds(group * TILE, TILE)

    def x0_copy(d):
        return pltpu.make_async_remote_copy(
            src_ref=x0,
            dst_ref=in_x0.at[d - 1],
            send_sem=x0s_sem.at[d - 1],
            recv_sem=x0r_sem.at[d - 1],
            device_id={"domain": me - d},
        )

    def x_copy(step, part, d):
        return pltpu.make_async_remote_copy(
            src_ref=xs.at[step, part],
            dst_ref=in_x.at[step - 1, part, d - 1],
            send_sem=xs_sem.at[step - 1, part, d - 1],
            recv_sem=xr_sem.at[step - 1, part, d - 1],
            device_id={"domain": me - d},
        )

    def b_copy(step, part, d):
        return pltpu.make_async_remote_copy(
            src_ref=out_b.at[step, part, d - 1],
            dst_ref=in_b.at[step, part, d - 1],
            send_sem=bs_sem.at[step, part, d - 1],
            recv_sem=br_sem.at[step, part, d - 1],
            device_id={"domain": me + d},
        )

    if with_gram:
        (in_f, parts, in_r, out_g, in_g) = refs[24:29]
        (fs_sem, fr_sem, rs_sem, rr_sem, gs_sem, gr_sem) = refs[29:]
        far = (mine + 2) % 4
        near = mine + 1 - 2 * (mine % 2)
        cross = (near + 2) % 4

        def f_copy(index, part):
            return pltpu.make_async_remote_copy(
                src_ref=in_f.at[0, part] if index == 2 else xs.at[3, part],
                dst_ref=in_f.at[index, part],
                send_sem=fs_sem.at[index, part],
                recv_sem=fr_sem.at[index, part],
                device_id={"vec": far if index == 0 else near},
            )

    load_x.wait()
    for d in range(1, REACH + 1):

        @pl.when(me >= d)
        def _():
            x0_copy(d).start()

    both[...] = stacked(x0[...])
    xs[0, 0], xs[0, 1] = packed(x0[...])
    load_index.wait()
    load_tiles.wait()

    def add_before(slot, carry):
        before = index_s[0, slot]
        weight = (before >= 0).astype(F32)
        tiles[slot] = tiles[slot] + tiles[jnp.maximum(before, 0)] * weight
        return carry

    lax.fori_loop(0, tiles.shape[0], add_before, 0)

    def block_at(row, col):
        slot = index_s[1, row * span + col]
        return tiles[jnp.maximum(slot, 0)] * (slot >= 0).astype(F32)

    def put(high, low, index, row, col, value):
        high[index, rows_at(row), rows_at(col)], low[index, rows_at(row), rows_at(col)] = halves(value)

    for d in range(1, REACH + 1):
        for row in range(groups):
            for col in range(groups):
                block = block_at(row, d * groups + col)
                put(fwd_h, fwd_l, d, row, col, block)
                put(back_h, back_l, d - 1, col, row, block.T)

        @pl.when(me + d < n)
        def _():
            first, second = packed(product(back_h[d - 1], back_l[d - 1], both[...]))
            out_b[0, 0, d - 1] = first
            b_copy(0, 0, d).start()
            out_b[0, 1, d - 1] = second
            b_copy(0, 1, d).start()

    for row in range(groups):
        for col in range(row, groups):
            block = block_at(row, col)
            if row == col:
                put(fwd_h, fwd_l, 0, row, col, 0.5 * (block + block.T))
            else:
                put(fwd_h, fwd_l, 0, row, col, block)
                put(fwd_h, fwd_l, 0, col, row, block.T)

    acc[0], acc[1] = packed(product(fwd_h[0], fwd_l[0], both[...]))
    for d in range(1, REACH + 1):

        @pl.when(me + d < n)
        def _():
            x0_copy(d).wait_recv()
            first, second = packed(product(fwd_h[d], fwd_l[d], stacked(in_x0[d - 1])))
            acc[0] += first
            acc[1] += second

    def add_back(step, part):
        for d in range(1, REACH + 1):

            @pl.when(me >= d)
            def _():
                b_copy(step, part, d).wait_recv()
                acc[part] += in_b[step, part, d - 1]

    def start_step(step, part):
        for d in range(1, REACH + 1):

            @pl.when(me >= d)
            def _():
                x_copy(step, part, d).start()

        put_stacked(both_half, 0, xs[step, part])
        for d in range(1, REACH + 1):

            @pl.when(me + d < n)
            def _():
                out_b[step, part, d - 1] = packed_product(back_h[d - 1], back_l[d - 1], both_half[...])
                b_copy(step, part, d).start()

        acc[part] = packed_product(fwd_h[0], fwd_l[0], both_half[...])

    def first_step(part, carry):
        add_back(0, part)
        xs[1, part] = (acc[part] - center_shift * xs[0, part]) / half_width
        start_step(1, part)
        return carry

    lax.fori_loop(0, 2, first_step, 0)

    def later_step(turn, carry):
        step, part = 1 + turn // 2, turn % 2
        for d in range(1, REACH + 1):

            @pl.when(me + d < n)
            def _():
                x_copy(step, part, d).wait_recv()
                put_stacked(both_half, 0, in_x[step - 1, part, d - 1])
                acc[part] += packed_product(fwd_h[d], fwd_l[d], both_half[...])

        add_back(step, part)
        xs[step + 1, part] = 2.0 * (acc[part] - center_shift * xs[step, part]) / half_width - xs[step - 1, part]

        @pl.when(turn < 2)
        def _():
            start_step(step + 1, part)

        if with_gram:

            @pl.when(turn >= 2)
            def _():
                f_copy(0, part).start()
                f_copy(1, part).start()

        return carry

    lax.fori_loop(0, 4, later_step, 0)
    f_ref[:half], f_ref[half:] = unpacked(xs[3, 0], xs[3, 1])

    if with_gram:
        left_h, left_l = back_h.at[0, :width], back_l.at[0, :width]
        left_h[...], left_l[...] = halves(f_ref[...].T)
        total = rows * n
        piece = width // n

        def r_copy(column, d):
            return pltpu.make_async_remote_copy(
                src_ref=parts.at[column, (me + d) % n],
                dst_ref=in_r.at[column, d],
                send_sem=rs_sem.at[column, d],
                recv_sem=rr_sem.at[column, d],
                device_id={"domain": (me + d) % n},
            )

        def g_copy(column, d):
            return pltpu.make_async_remote_copy(
                src_ref=out_g.at[column],
                dst_ref=in_g.at[column, d],
                send_sem=gs_sem.at[column, d],
                recv_sem=gr_sem.at[column, d],
                device_id={"domain": (me + d) % n},
            )

        def multiply(column, first, second):
            put_stacked(both, 0, first)
            put_stacked(both, 1, second)
            wide = jnp.dot(left_h[...], both[...], preferred_element_type=F32)
            wide = wide + jnp.dot(left_l[...], both[...], preferred_element_type=F32)
            first, second = wide[:, :width], wide[:, width:]
            first, second = first + swapped(first), second + swapped(second)
            block = jnp.where(left_lanes(first), first, second) / total
            parts[column] = block.reshape(n, piece, width)
            for d in range(1, n):
                r_copy(column, d).start()

        def add_up(column):
            block = parts[column, me]
            for d in range(1, n):
                r_copy(column, d).wait_recv()
                block = block + in_r[column, d]
            out_g[column] = block
            for d in range(1, n):
                g_copy(column, d).start()

        def put_rows(owner, first, second, one, other):
            here = pl.ds(pl.multiple_of(owner * piece, piece), piece)
            first, second = unpacked(first, second)
            g_ref[here, pl.ds(pl.multiple_of(one * width, width), width)] = first
            g_ref[here, pl.ds(pl.multiple_of(other * width, width), width)] = second

        def collect(column, one, other):
            put_rows(me, out_g[column], out_g[column + 2], one, other)
            for d in range(1, n):
                g_copy(column, d).wait_recv()
                g_copy(column + 2, d).wait_recv()
                put_rows((me + n - d) % n, in_g[column, d], in_g[column + 2, d], one, other)

        f_copy(1, 0).wait_recv()
        multiply(0, xs[3, 0], in_f[1, 0])
        f_copy(0, 0).wait_recv()
        f_copy(2, 0).start()
        f_copy(1, 1).wait_recv()
        multiply(2, xs[3, 1], in_f[1, 1])
        f_copy(2, 0).wait_recv()
        multiply(1, in_f[0, 0], in_f[2, 0])
        f_copy(0, 1).wait_recv()
        f_copy(2, 1).start()
        f_copy(2, 1).wait_recv()
        multiply(3, in_f[0, 1], in_f[2, 1])
        add_up(0)
        add_up(2)
        add_up(1)
        add_up(3)
        collect(0, mine, near)
        collect(1, far, cross)
        for index in range(3):
            for part in range(2):
                f_copy(index, part).wait_send()
        for column in range(4):
            for d in range(1, n):
                r_copy(column, d).wait_send()
                g_copy(column, d).wait_send()

    for d in range(1, REACH + 1):

        @pl.when(me >= d)
        def _():
            x0_copy(d).wait_send()
            for step in range(1, 3):
                for part in range(2):
                    x_copy(step, part, d).wait_send()

        @pl.when(me + d < n)
        def _():
            for step in range(3):
                for part in range(2):
                    b_copy(step, part, d).wait_send()


def shards(vectors, hamiltonian, tile_pairs, tile_counts):
    n = lax.axis_size("domain")
    m = lax.axis_size("vec")
    rows, width = vectors.shape
    groups = rows // TILE
    half = rows // 2
    slots = tile_pairs.shape[0]
    lanes = -(-max(slots, (REACH + 1) * groups * groups) // 128) * 128
    with_gram = m == 4 and n % 2 == 0 and width % (8 * n) == 0
    dma = pltpu.SemaphoreType.DMA
    out_shape = [jax.ShapeDtypeStruct((rows, width), F32)]
    scratch = [
        pltpu.VMEM(hamiltonian.shape, F32),
        pltpu.VMEM((rows, width), F32),
        pltpu.VMEM((2, slots), jnp.int32),
        pltpu.VMEM((2, lanes), jnp.int32),
        pltpu.SMEM((2, lanes), jnp.int32),
        pltpu.VMEM((REACH + 1, rows, rows), BF16),
        pltpu.VMEM((REACH + 1, rows, rows), BF16),
        pltpu.VMEM((REACH, rows, rows), BF16),
        pltpu.VMEM((REACH, rows, rows), BF16),
        pltpu.VMEM((rows, 2 * width), BF16),
        pltpu.VMEM((rows, width), BF16),
        pltpu.VMEM((2, half, width), F32),
        pltpu.VMEM((4, 2, half, width), F32),
        pltpu.VMEM((REACH, rows, width), F32),
        pltpu.VMEM((2, 2, REACH, half, width), F32),
        pltpu.VMEM((3, 2, REACH, half, width), F32),
        pltpu.VMEM((3, 2, REACH, half, width), F32),
        dma((4,)),
        dma((REACH,)),
        dma((REACH,)),
        dma((2, 2, REACH)),
        dma((2, 2, REACH)),
        dma((3, 2, REACH)),
        dma((3, 2, REACH)),
    ]
    if with_gram:
        out_shape.append(jax.ShapeDtypeStruct((width, m * width), F32))
        scratch += [
            pltpu.VMEM((3, 2, half, width), F32),
            pltpu.VMEM((m, n, width // n, width), F32),
            pltpu.VMEM((m, n, width // n, width), F32),
            pltpu.VMEM((m, width // n, width), F32),
            pltpu.VMEM((m, n, width // n, width), F32),
            dma((3, 2)),
            dma((3, 2)),
            dma((m, n)),
            dma((m, n)),
            dma((m, n)),
            dma((m, n)),
        ]
    outs = pl.pallas_call(
        functools.partial(filter_kernel, n, m, with_gram),
        out_shape=out_shape,
        in_specs=[
            pl.BlockSpec(memory_space=pltpu.HBM),
            pl.BlockSpec(memory_space=pltpu.HBM),
            pl.BlockSpec(memory_space=pltpu.SMEM),
            pl.BlockSpec(memory_space=pltpu.HBM),
        ],
        out_specs=[pl.BlockSpec(memory_space=pltpu.VMEM)] * len(out_shape),
        scratch_shapes=scratch,
        compiler_params=pltpu.CompilerParams(
            collective_id=0, has_side_effects=True, vmem_limit_bytes=52 * 2**20
        ),
        name="chebyshev",
    )(vectors, tile_pairs.T, tile_counts, hamiltonian)
    if with_gram:
        return tuple(outs)
    (filtered,) = outs
    gathered = lax.all_gather(filtered, "vec", axis=1, tiled=True)
    partial_block = jnp.dot(
        filtered.T, gathered, precision=lax.Precision.HIGHEST, preferred_element_type=F32
    ) / (rows * n)
    return (filtered, lax.psum(partial_block, "domain"))


def solution(mesh):
    in_specs = (P("domain", "vec"), P("domain", None, None), P("domain", None), P("domain"))
    out_specs = (P("domain", "vec"), P("vec", None))
    return jax.shard_map(shards, mesh=mesh, in_specs=in_specs, out_specs=out_specs, check_vma=False)
```

```python
import functools

import jax
import jax.numpy as jnp
from jax import lax
from jax.experimental import pallas as pl
from jax.experimental.pallas import tpu as pltpu
from jax.sharding import PartitionSpec as P

TILE = 128
REACH = 2

center_shift = 1.0
half_width = 1.5

F32 = jnp.float32
BF16 = jnp.bfloat16


def halves(value):
    high = value.astype(BF16)
    low = (value - high.astype(F32)).astype(BF16)
    return high, low


def stacked(value):
    return jnp.concatenate(halves(value), 1)


def left_lanes(value):
    return lax.broadcasted_iota(jnp.int32, value.shape, 1) < value.shape[1] // 2


def swapped(value):
    return pltpu.roll(value, value.shape[1] // 2, 1)


def packed(value):
    upper, lower = value[: value.shape[0] // 2], value[value.shape[0] // 2 :]
    left = left_lanes(upper)
    return jnp.where(left, upper, swapped(lower)), jnp.where(left, swapped(upper), lower)


def unpacked(first, second):
    left = left_lanes(first)
    return jnp.where(left, first, swapped(second)), jnp.where(left, swapped(first), second)


def product(high, low, both):
    wide = jnp.dot(high, both, preferred_element_type=F32)
    wide = wide + jnp.dot(low, both, preferred_element_type=F32)
    width = both.shape[1] // 2
    return wide[:, :width] + wide[:, width:]


def packed_product(high, low, both):
    wide = jnp.dot(high, both, preferred_element_type=F32)
    wide = wide + jnp.dot(low, both, preferred_element_type=F32)
    wide = wide + swapped(wide)
    half = wide.shape[0] // 2
    return jnp.where(left_lanes(wide[:half]), wide[:half], wide[half:])


def put_stacked(both, at, value):
    high = value.astype(BF16).astype(F32)
    low = value - high
    left = left_lanes(value)
    half, width = value.shape
    columns = pl.ds(at * width, width)
    both[:half, columns] = jnp.where(left, high, swapped(low)).astype(BF16)
    both[half:, columns] = jnp.where(left, swapped(high), low).astype(BF16)


def put_index(groups, me, pairs, count, index_ref):
    slots = pairs.shape[1]
    span = (REACH + 1) * groups
    lanes = index_ref.shape[1]
    code = (pairs[0:1] - me * groups) * span + pairs[1:2] - me * groups
    row = lax.broadcasted_iota(jnp.int32, (slots, slots), 0)
    lane = lax.broadcasted_iota(jnp.int32, (slots, slots), 1)
    down = jnp.sum(jnp.where(row == lane, code, 0), axis=1, keepdims=True)
    same = (down == code) & (row < lane) & (lane < count)
    index_ref[0:1, :slots] = jnp.max(jnp.where(same, row, -1), axis=0, keepdims=True)
    row = lax.broadcasted_iota(jnp.int32, (slots, lanes), 0)
    lane = lax.broadcasted_iota(jnp.int32, (slots, lanes), 1)
    here = (down == lane) & (row < count)
    index_ref[1:2] = jnp.max(jnp.where(here, row, -1), axis=0, keepdims=True)


def filter_kernel(n, m, with_gram, x_ref, pairs_ref, count_ref, ham_ref, *refs):
    if with_gram:
        f_ref, g_ref, *refs = refs
    else:
        f_ref, *refs = refs
    (tiles, x0, pairs, index_v, index_s, fwd_h, fwd_l, back_h, back_l, both, both_half) = refs[:11]
    (acc, xs, in_x, in_b, out_b) = refs[11:16]
    (load_sem, xs_sem, xr_sem, bs_sem, br_sem) = refs[16:21]
    me = lax.axis_index("domain")
    mine = lax.axis_index("vec")
    rows, width = x_ref.shape
    half = rows // 2
    groups = rows // TILE
    span = (REACH + 1) * groups

    load_pairs = pltpu.make_async_copy(pairs_ref, pairs, load_sem.at[0])
    load_pairs.start()
    load_x = pltpu.make_async_copy(x_ref, x0, load_sem.at[1])
    load_x.start()
    load_tiles = pltpu.make_async_copy(ham_ref, tiles, load_sem.at[2])
    load_tiles.start()

    barrier = pltpu.get_barrier_semaphore()
    if with_gram:
        for d in range(1, n):
            pl.semaphore_signal(barrier, inc=1, device_id={"domain": (me + d) % n})
        for d in range(1, m):
            pl.semaphore_signal(barrier, inc=1, device_id={"vec": (mine + d) % m})
    else:
        for d in range(1, REACH + 1):

            @pl.when(me >= d)
            def _():
                pl.semaphore_signal(barrier, inc=1, device_id={"domain": me - d})

            @pl.when(me + d < n)
            def _():
                pl.semaphore_signal(barrier, inc=1, device_id={"domain": me + d})

    load_pairs.wait()
    put_index(groups, me, pairs[...], count_ref[0], index_v)
    load_index = pltpu.make_async_copy(index_v, index_s, load_sem.at[3])
    load_index.start()

    def rows_at(group):
        return pl.ds(group * TILE, TILE)

    def x_copy(step, part, d):
        return pltpu.make_async_remote_copy(
            src_ref=xs.at[step, part],
            dst_ref=in_x.at[step, part, d - 1],
            send_sem=xs_sem.at[step, part, d - 1],
            recv_sem=xr_sem.at[step, part, d - 1],
            device_id={"domain": me - d},
        )

    def b_copy(step, part, d):
        return pltpu.make_async_remote_copy(
            src_ref=out_b.at[step, part, d - 1],
            dst_ref=in_b.at[step, part, d - 1],
            send_sem=bs_sem.at[step, part, d - 1],
            recv_sem=br_sem.at[step, part, d - 1],
            device_id={"domain": me + d},
        )

    if with_gram:
        (in_f, parts, in_r, in_g, out_t, in_t) = refs[21:27]
        (fs_sem, fr_sem, rs_sem, rr_sem, gs_sem, gr_sem, ts_sem, tr_sem) = refs[27:]
        far = (mine + 2) % 4
        near = mine + 1 - 2 * (mine % 2)
        cross = (near + 2) % 4

        def f_copy(index, part):
            return pltpu.make_async_remote_copy(
                src_ref=in_f.at[0, part] if index == 2 else xs.at[3, part],
                dst_ref=in_f.at[index, part],
                send_sem=fs_sem.at[index, part],
                recv_sem=fr_sem.at[index, part],
                device_id={"vec": far if index == 0 else near},
            )

    load_x.wait()
    both[...] = stacked(x0[...])
    xs[0, 0], xs[0, 1] = packed(x0[...])
    load_index.wait()
    load_tiles.wait()

    def add_before(slot, carry):
        before = index_s[0, slot]
        weight = (before >= 0).astype(F32)
        tiles[slot] = tiles[slot] + tiles[jnp.maximum(before, 0)] * weight
        return carry

    lax.fori_loop(0, tiles.shape[0], add_before, 0, unroll=4)

    if with_gram:
        pl.semaphore_wait(barrier, n - 1 + m - 1)
    else:
        for d in range(1, REACH + 1):

            @pl.when(me >= d)
            def _():
                pl.semaphore_wait(barrier, 1)

            @pl.when(me + d < n)
            def _():
                pl.semaphore_wait(barrier, 1)

    def send_x(step, part):
        for d in range(1, REACH + 1):

            @pl.when(me >= d)
            def _():
                x_copy(step, part, d).start()

    send_x(0, 0)
    send_x(0, 1)

    def block_at(row, col):
        slot = index_s[1, row * span + col]
        return tiles[jnp.maximum(slot, 0)] * (slot >= 0).astype(F32)

    def put(high, low, index, row, col, value):
        high[index, rows_at(row), rows_at(col)], low[index, rows_at(row), rows_at(col)] = halves(value)

    for d in range(1, REACH + 1):
        for row in range(groups):
            for col in range(groups):
                block = block_at(row, d * groups + col)
                put(fwd_h, fwd_l, d, row, col, block)
                put(back_h, back_l, d - 1, col, row, block.T)

        @pl.when(me + d < n)
        def _():
            first, second = packed(product(back_h[d - 1], back_l[d - 1], both[...]))
            out_b[0, 0, d - 1] = first
            out_b[0, 1, d - 1] = second
            b_copy(0, 0, d).start()

    for d in range(1, REACH + 1):

        @pl.when(me + d < n)
        def _():
            b_copy(0, 1, d).start()

    for row in range(groups):
        for col in range(row, groups):
            block = block_at(row, col)
            if row == col:
                put(fwd_h, fwd_l, 0, row, col, 0.5 * (block + block.T))
            else:
                put(fwd_h, fwd_l, 0, row, col, block)
                put(fwd_h, fwd_l, 0, col, row, block.T)

    acc[0], acc[1] = packed(product(fwd_h[0], fwd_l[0], both[...]))
    def add_back(step, part):
        for d in range(1, REACH + 1):

            @pl.when(me >= d)
            def _():
                b_copy(step, part, d).wait_recv()
                acc[part] += in_b[step, part, d - 1]

    def start_step(step, part):
        send_x(step, part)
        put_stacked(both_half, 0, xs[step, part])
        for d in range(1, REACH + 1):

            @pl.when(me + d < n)
            def _():
                out_b[step, part, d - 1] = packed_product(back_h[d - 1], back_l[d - 1], both_half[...])
                b_copy(step, part, d).start()

        acc[part] = packed_product(fwd_h[0], fwd_l[0], both_half[...])

    def one_turn(turn, carry):
        step, part = turn // 2, turn % 2
        for d in range(1, REACH + 1):

            @pl.when(me + d < n)
            def _():
                x_copy(step, part, d).wait_recv()
                put_stacked(both_half, 0, in_x[step, part, d - 1])
                acc[part] += packed_product(fwd_h[d], fwd_l[d], both_half[...])

        add_back(step, part)
        later = (step > 0).astype(F32)
        change = (1.0 + later) * (acc[part] - center_shift * xs[step, part]) / half_width
        xs[step + 1, part] = change - later * xs[jnp.maximum(step - 1, 0), part]

        @pl.when(turn < 4)
        def _():
            start_step(step + 1, part)

        if with_gram:

            @pl.when(turn >= 4)
            def _():
                f_copy(0, part).start()
                f_copy(1, part).start()

        return carry

    lax.fori_loop(0, 6, one_turn, 0)
    f_ref[:half], f_ref[half:] = unpacked(xs[3, 0], xs[3, 1])

    if with_gram:
        left_h, left_l = back_h.at[0, :width], back_l.at[0, :width]
        left_h[...], left_l[...] = halves(f_ref[...].T)
        total = rows * n
        owners, first_owner = n // 2, n // 4
        owner = jnp.clip(me - first_owner, 0, owners - 1)
        owns = (me >= first_owner) & (me < first_owner + owners)
        sizes = [width // owners] * 3 + [width // n]
        mid = width // 2

        def rows_of(stage):
            return pl.ds(sum(sizes[:stage]), sizes[stage])

        def r_copy(stage, target, source):
            return pltpu.make_async_remote_copy(
                src_ref=parts.at[target, rows_of(stage)],
                dst_ref=in_r.at[source, rows_of(stage)],
                send_sem=rs_sem.at[stage, target],
                recv_sem=rr_sem.at[stage, source],
                device_id={"domain": first_owner + target},
            )

        def g_copy(stage, source, d):
            return pltpu.make_async_remote_copy(
                src_ref=in_g.at[source, rows_of(stage)],
                dst_ref=in_g.at[source, rows_of(stage)],
                send_sem=gs_sem.at[stage, d],
                recv_sem=gr_sem.at[stage, source],
                device_id={"domain": (me + d) % n},
            )

        def scatter(stage, block):
            parts[:, rows_of(stage)] = (block / total).reshape(owners, sizes[stage], width)
            for target in range(owners):

                @pl.when(me != first_owner + target)
                def _():
                    r_copy(stage, target, me).start()

        def multiply(stage, top, first, second):
            put_stacked(both, 0, first)
            put_stacked(both, 1, second)
            wide = jnp.dot(left_h[top:], both[...], preferred_element_type=F32)
            wide = wide + jnp.dot(left_l[top:], both[...], preferred_element_type=F32)
            first, second = wide[:, :width], wide[:, width:]
            first, second = first + swapped(first), second + swapped(second)
            scatter(stage, jnp.where(left_lanes(first), first, second))

        def add_up(stage):
            @pl.when(owns)
            def _():
                block = parts[owner, rows_of(stage)]
                for d in range(1, n):
                    source = (me + d) % n
                    r_copy(stage, owner, source).wait_recv()
                    block = block + in_r[source, rows_of(stage)]
                in_g[owner, rows_of(stage)] = block
                for d in range(1, n):
                    g_copy(stage, owner, d).start()

        def collected(stage):
            for source in range(owners):

                @pl.when(me != first_owner + source)
                def _():
                    g_copy(stage, source, 1).wait_recv()

            return in_g[:, rows_of(stage)].reshape(owners * sizes[stage], width)

        def columns_of(source):
            return pl.ds(pl.multiple_of(source * width, width), width)

        def t_copy(index):
            return pltpu.make_async_remote_copy(
                src_ref=out_t,
                dst_ref=in_t.at[index],
                send_sem=ts_sem.at[index],
                recv_sem=tr_sem.at[index],
                device_id={"vec": cross if index else far},
            )

        def turned(index):
            t_copy(index).wait_recv()
            return jnp.concatenate([in_t[index], in_t[index]], 0).T

        f_copy(0, 0).wait_recv()
        f_copy(2, 0).start()
        f_copy(2, 0).wait_recv()
        multiply(2, 0, in_f[0, 0], in_f[2, 0])
        f_copy(1, 0).wait_recv()
        multiply(0, 0, xs[3, 0], in_f[1, 0])
        f_copy(1, 1).wait_recv()
        multiply(1, 0, xs[3, 1], in_f[1, 1])
        f_copy(0, 1).wait_recv()
        f_copy(2, 1).start()
        f_copy(2, 1).wait_recv()
        multiply(3, mid, in_f[0, 1], in_f[2, 1])
        for stage in (2, 0, 1, 3):
            add_up(stage)
        block = collected(2)
        out_t[...] = block[mid:]
        t_copy(0).start()
        t_copy(1).start()
        first, second = unpacked(collected(0), collected(1))
        g_ref[:, columns_of(mine)] = first
        g_ref[:, columns_of(near)] = second
        upper, lower = block[:mid], block[mid:]
        left = left_lanes(upper)
        g_ref[:mid, columns_of(far)] = jnp.where(left, upper, turned(0)[:mid])
        g_ref[:mid, columns_of(cross)] = jnp.where(left, swapped(upper), turned(1)[mid:])
        last = collected(3)
        g_ref[mid:, columns_of(far)] = jnp.where(left, lower, swapped(last))
        g_ref[mid:, columns_of(cross)] = jnp.where(left, swapped(lower), last)
        t_copy(0).wait_send()
        t_copy(1).wait_send()
        for index in range(3):
            for part in range(2):
                f_copy(index, part).wait_send()
        for stage in range(4):
            for target in range(owners):

                @pl.when(me != first_owner + target)
                def _():
                    r_copy(stage, target, me).wait_send()

        @pl.when(owns)
        def _():
            for stage in range(4):
                for d in range(1, n):
                    g_copy(stage, owner, d).wait_send()

    for d in range(1, REACH + 1):

        @pl.when(me >= d)
        def _():
            for step in range(3):
                for part in range(2):
                    x_copy(step, part, d).wait_send()

        @pl.when(me + d < n)
        def _():
            for step in range(3):
                for part in range(2):
                    b_copy(step, part, d).wait_send()


def shards(vectors, hamiltonian, tile_pairs, tile_counts):
    n = lax.axis_size("domain")
    m = lax.axis_size("vec")
    rows, width = vectors.shape
    groups = rows // TILE
    half = rows // 2
    slots = tile_pairs.shape[0]
    lanes = -(-max(slots, (REACH + 1) * groups * groups) // 128) * 128
    with_gram = m == 4 and n % 4 == 0 and width % (8 * n) == 0
    dma = pltpu.SemaphoreType.DMA
    out_shape = [jax.ShapeDtypeStruct((rows, width), F32)]
    scratch = [
        pltpu.VMEM(hamiltonian.shape, F32),
        pltpu.VMEM((rows, width), F32),
        pltpu.VMEM((2, slots), jnp.int32),
        pltpu.VMEM((2, lanes), jnp.int32),
        pltpu.SMEM((2, lanes), jnp.int32),
        pltpu.VMEM((REACH + 1, rows, rows), BF16),
        pltpu.VMEM((REACH + 1, rows, rows), BF16),
        pltpu.VMEM((REACH, rows, rows), BF16),
        pltpu.VMEM((REACH, rows, rows), BF16),
        pltpu.VMEM((rows, 2 * width), BF16),
        pltpu.VMEM((rows, width), BF16),
        pltpu.VMEM((2, half, width), F32),
        pltpu.VMEM((4, 2, half, width), F32),
        pltpu.VMEM((3, 2, REACH, half, width), F32),
        pltpu.VMEM((3, 2, REACH, half, width), F32),
        pltpu.VMEM((3, 2, REACH, half, width), F32),
        dma((4,)),
        dma((3, 2, REACH)),
        dma((3, 2, REACH)),
        dma((3, 2, REACH)),
        dma((3, 2, REACH)),
    ]
    if with_gram:
        out_shape.append(jax.ShapeDtypeStruct((width, m * width), F32))
        scratch += [
            pltpu.VMEM((3, 2, half, width), F32),
            pltpu.VMEM((n // 2, 7 * width // n, width), F32),
            pltpu.VMEM((n, 7 * width // n, width), F32),
            pltpu.VMEM((n // 2, 7 * width // n, width), F32),
            pltpu.VMEM((width // 2, width), F32),
            pltpu.VMEM((2, width // 2, width), F32),
            dma((3, 2)),
            dma((3, 2)),
            dma((4, n // 2)),
            dma((4, n)),
            dma((4, n)),
            dma((4, n // 2)),
            dma((2,)),
            dma((2,)),
        ]
    outs = pl.pallas_call(
        functools.partial(filter_kernel, n, m, with_gram),
        out_shape=out_shape,
        in_specs=[
            pl.BlockSpec(memory_space=pltpu.HBM),
            pl.BlockSpec(memory_space=pltpu.HBM),
            pl.BlockSpec(memory_space=pltpu.SMEM),
            pl.BlockSpec(memory_space=pltpu.HBM),
        ],
        out_specs=[pl.BlockSpec(memory_space=pltpu.VMEM)] * len(out_shape),
        scratch_shapes=scratch,
        compiler_params=pltpu.CompilerParams(
            collective_id=0, has_side_effects=True, vmem_limit_bytes=52 * 2**20
        ),
        name="chebyshev",
    )(pltpu.with_memory_space_constraint(vectors, pltpu.HBM), pltpu.with_memory_space_constraint(tile_pairs.T, pltpu.HBM), tile_counts, hamiltonian)
    if with_gram:
        return tuple(outs)
    (filtered,) = outs
    gathered = lax.all_gather(filtered, "vec", axis=1, tiled=True)
    partial_block = jnp.dot(
        filtered.T, gathered, precision=lax.Precision.HIGHEST, preferred_element_type=F32
    ) / (rows * n)
    return (filtered, lax.psum(partial_block, "domain"))


def solution(mesh):
    in_specs = (P("domain", "vec"), P("domain", None, None), P("domain", None), P("domain"))
    out_specs = (P("domain", "vec"), P("vec", None))
    return jax.shard_map(shards, mesh=mesh, in_specs=in_specs, out_specs=out_specs, check_vma=False)
```

```python
import functools

import jax
import jax.numpy as jnp
from jax import lax
from jax.experimental import pallas as pl
from jax.experimental.pallas import tpu as pltpu
from jax.sharding import PartitionSpec as P

TILE = 128
REACH = 2

center_shift = 1.0
half_width = 1.5

F32 = jnp.float32
BF16 = jnp.bfloat16


def halves(value):
    high = value.astype(BF16)
    low = (value - high.astype(F32)).astype(BF16)
    return high, low


def stacked(value):
    return jnp.concatenate(halves(value), 1)


def left_lanes(value):
    return lax.broadcasted_iota(jnp.int32, value.shape, 1) < value.shape[1] // 2


def swapped(value):
    return pltpu.roll(value, value.shape[1] // 2, 1)


def packed(value):
    upper, lower = value[: value.shape[0] // 2], value[value.shape[0] // 2 :]
    left = left_lanes(upper)
    return jnp.where(left, upper, swapped(lower)), jnp.where(left, swapped(upper), lower)


def unpacked(first, second):
    left = left_lanes(first)
    return jnp.where(left, first, swapped(second)), jnp.where(left, swapped(first), second)


def product(high, low, both):
    wide = jnp.dot(high, both, preferred_element_type=F32)
    wide = wide + jnp.dot(low, both, preferred_element_type=F32)
    width = both.shape[1] // 2
    return wide[:, :width] + wide[:, width:]


def packed_product(high, low, both):
    wide = jnp.dot(high, both, preferred_element_type=F32)
    wide = wide + jnp.dot(low, both, preferred_element_type=F32)
    wide = wide + swapped(wide)
    half = wide.shape[0] // 2
    return jnp.where(left_lanes(wide[:half]), wide[:half], wide[half:])


def put_stacked(both, at, value):
    high = value.astype(BF16).astype(F32)
    low = value - high
    left = left_lanes(value)
    half, width = value.shape
    columns = pl.ds(at * width, width)
    both[:half, columns] = jnp.where(left, high, swapped(low)).astype(BF16)
    both[half:, columns] = jnp.where(left, swapped(high), low).astype(BF16)


def put_index(groups, me, pairs, count, index_ref):
    slots = pairs.shape[1]
    span = (REACH + 1) * groups
    lanes = index_ref.shape[1]
    code = (pairs[0:1] - me * groups) * span + pairs[1:2] - me * groups
    row = lax.broadcasted_iota(jnp.int32, (slots, slots), 0)
    lane = lax.broadcasted_iota(jnp.int32, (slots, slots), 1)
    down = jnp.sum(jnp.where(row == lane, code, 0), axis=1, keepdims=True)
    same = (down == code) & (row < lane) & (lane < count)
    index_ref[0:1, :slots] = jnp.max(jnp.where(same, row, -1), axis=0, keepdims=True)
    row = lax.broadcasted_iota(jnp.int32, (slots, lanes), 0)
    lane = lax.broadcasted_iota(jnp.int32, (slots, lanes), 1)
    here = (down == lane) & (row < count)
    index_ref[1:2] = jnp.max(jnp.where(here, row, -1), axis=0, keepdims=True)


def filter_kernel(n, m, with_gram, x_ref, pairs_ref, count_ref, ham_ref, *refs):
    if with_gram:
        f_ref, g_ref, *refs = refs
    else:
        f_ref, *refs = refs
    (tiles, x0, pairs, index_v, index_s, fwd_h, fwd_l, back_h, back_l, both, both_half) = refs[:11]
    (acc, xs, in_x, in_b, out_b) = refs[11:16]
    (load_sem, xs_sem, xr_sem, bs_sem, br_sem) = refs[16:21]
    me = lax.axis_index("domain")
    mine = lax.axis_index("vec")
    rows, width = x_ref.shape
    half = rows // 2
    groups = rows // TILE
    span = (REACH + 1) * groups

    load_pairs = pltpu.make_async_copy(pairs_ref, pairs, load_sem.at[0])
    load_pairs.start()
    load_x = pltpu.make_async_copy(x_ref, x0, load_sem.at[1])
    load_x.start()
    load_tiles = pltpu.make_async_copy(ham_ref, tiles, load_sem.at[2])
    load_tiles.start()

    barrier = pltpu.get_barrier_semaphore()
    if with_gram:
        for d in range(1, n):
            pl.semaphore_signal(barrier, inc=1, device_id={"domain": (me + d) % n})
        for d in range(1, m):
            pl.semaphore_signal(barrier, inc=1, device_id={"vec": (mine + d) % m})
    else:
        for d in range(1, REACH + 1):

            @pl.when(me >= d)
            def _():
                pl.semaphore_signal(barrier, inc=1, device_id={"domain": me - d})

            @pl.when(me + d < n)
            def _():
                pl.semaphore_signal(barrier, inc=1, device_id={"domain": me + d})

    load_pairs.wait()
    put_index(groups, me, pairs[...], count_ref[0], index_v)
    load_index = pltpu.make_async_copy(index_v, index_s, load_sem.at[3])
    load_index.start()

    def rows_at(group):
        return pl.ds(group * TILE, TILE)

    def x_copy(step, part, d):
        return pltpu.make_async_remote_copy(
            src_ref=xs.at[step, part],
            dst_ref=in_x.at[step, part, d - 1],
            send_sem=xs_sem.at[step, part, d - 1],
            recv_sem=xr_sem.at[step, part, d - 1],
            device_id={"domain": me - d},
        )

    def b_copy(step, part, d):
        return pltpu.make_async_remote_copy(
            src_ref=out_b.at[step, part, d - 1],
            dst_ref=in_b.at[step, part, d - 1],
            send_sem=bs_sem.at[step, part, d - 1],
            recv_sem=br_sem.at[step, part, d - 1],
            device_id={"domain": me + d},
        )

    if with_gram:
        (in_f, parts, in_r, in_g, out_t, in_t) = refs[21:27]
        (fs_sem, fr_sem, rs_sem, rr_sem, gs_sem, gr_sem, ts_sem, tr_sem) = refs[27:]
        far = (mine + 2) % 4
        near = mine + 1 - 2 * (mine % 2)
        cross = (near + 2) % 4

        def f_copy(index, part):
            return pltpu.make_async_remote_copy(
                src_ref=in_f.at[0, part] if index == 2 else xs.at[3, part],
                dst_ref=in_f.at[index, part],
                send_sem=fs_sem.at[index, part],
                recv_sem=fr_sem.at[index, part],
                device_id={"vec": far if index == 0 else near},
            )

    load_x.wait()
    both[...] = stacked(x0[...])
    xs[0, 0], xs[0, 1] = packed(x0[...])
    load_index.wait()
    load_tiles.wait()

    def add_before(slot, carry):
        before = index_s[0, slot]
        weight = (before >= 0).astype(F32)
        tiles[slot] = tiles[slot] + tiles[jnp.maximum(before, 0)] * weight
        return carry

    lax.fori_loop(0, tiles.shape[0], add_before, 0, unroll=4)

    if with_gram:
        pl.semaphore_wait(barrier, n - 1 + m - 1)
    else:
        for d in range(1, REACH + 1):

            @pl.when(me >= d)
            def _():
                pl.semaphore_wait(barrier, 1)

            @pl.when(me + d < n)
            def _():
                pl.semaphore_wait(barrier, 1)

    def send_x(step, part):
        for d in range(1, REACH + 1):

            @pl.when(me >= d)
            def _():
                x_copy(step, part, d).start()

    send_x(0, 0)
    send_x(0, 1)

    def block_at(row, col):
        slot = index_s[1, row * span + col]
        return tiles[jnp.maximum(slot, 0)] * (slot >= 0).astype(F32)

    def put(high, low, index, row, col, value):
        high[index, rows_at(row), rows_at(col)], low[index, rows_at(row), rows_at(col)] = halves(value)

    for d in range(1, REACH + 1):
        for row in range(groups):
            for col in range(groups):
                block = block_at(row, d * groups + col)
                put(fwd_h, fwd_l, d, row, col, block)
                put(back_h, back_l, d - 1, col, row, block.T)

        @pl.when(me + d < n)
        def _():
            first, second = packed(product(back_h[d - 1], back_l[d - 1], both[...]))
            out_b[0, 0, d - 1] = first
            out_b[0, 1, d - 1] = second
            b_copy(0, 0, d).start()

    for d in range(1, REACH + 1):

        @pl.when(me + d < n)
        def _():
            b_copy(0, 1, d).start()

    for row in range(groups):
        for col in range(row, groups):
            block = block_at(row, col)
            if row == col:
                put(fwd_h, fwd_l, 0, row, col, 0.5 * (block + block.T))
            else:
                put(fwd_h, fwd_l, 0, row, col, block)
                put(fwd_h, fwd_l, 0, col, row, block.T)

    acc[0], acc[1] = packed(product(fwd_h[0], fwd_l[0], both[...]))
    def add_back(step, part):
        for d in range(1, REACH + 1):

            @pl.when(me >= d)
            def _():
                b_copy(step, part, d).wait_recv()
                acc[part] += in_b[step, part, d - 1]

    def start_step(step, part):
        send_x(step, part)
        put_stacked(both_half, 0, xs[step, part])
        for d in range(1, REACH + 1):

            @pl.when(me + d < n)
            def _():
                out_b[step, part, d - 1] = packed_product(back_h[d - 1], back_l[d - 1], both_half[...])
                b_copy(step, part, d).start()

        acc[part] = packed_product(fwd_h[0], fwd_l[0], both_half[...])

    def one_turn(turn, carry):
        step, part = turn // 2, turn % 2
        for d in range(1, REACH + 1):

            @pl.when(me + d < n)
            def _():
                x_copy(step, part, d).wait_recv()
                put_stacked(both_half, 0, in_x[step, part, d - 1])
                acc[part] += packed_product(fwd_h[d], fwd_l[d], both_half[...])

        add_back(step, part)
        later = (step > 0).astype(F32)
        change = (1.0 + later) * (acc[part] - center_shift * xs[step, part]) / half_width
        xs[step + 1, part] = change - later * xs[jnp.maximum(step - 1, 0), part]

        @pl.when(turn < 4)
        def _():
            start_step(step + 1, part)

        if with_gram:

            @pl.when(turn >= 4)
            def _():
                f_copy(0, part).start()
                f_copy(1, part).start()

        return carry

    lax.fori_loop(0, 6, one_turn, 0)
    f_ref[:half], f_ref[half:] = unpacked(xs[3, 0], xs[3, 1])

    if with_gram:
        left_h, left_l = back_h.at[0, :width], back_l.at[0, :width]
        left_h[...], left_l[...] = halves(f_ref[...].T)
        total = rows * n
        owners, first_owner = n // 2, n // 4
        owner = jnp.clip(me - first_owner, 0, owners - 1)
        owns = (me >= first_owner) & (me < first_owner + owners)
        sizes = [width // owners, width // n] * 2
        mid = width // 2

        def rows_of(stage):
            return pl.ds(sum(sizes[:stage]), sizes[stage])

        def r_copy(stage, target, source):
            return pltpu.make_async_remote_copy(
                src_ref=parts.at[target, rows_of(stage)],
                dst_ref=in_r.at[source, rows_of(stage)],
                send_sem=rs_sem.at[stage, target],
                recv_sem=rr_sem.at[stage, source],
                device_id={"domain": first_owner + target},
            )

        def g_copy(stage, source, d):
            return pltpu.make_async_remote_copy(
                src_ref=in_g.at[source, rows_of(stage)],
                dst_ref=in_g.at[source, rows_of(stage)],
                send_sem=gs_sem.at[stage, d],
                recv_sem=gr_sem.at[stage, source],
                device_id={"domain": (me + d) % n},
            )

        def scatter(stage, block):
            parts[:, rows_of(stage)] = (block / total).reshape(owners, sizes[stage], width)
            for target in range(owners):

                @pl.when(me != first_owner + target)
                def _():
                    r_copy(stage, target, me).start()

        def multiply(stage, top, first, second):
            put_stacked(both, 0, first)
            put_stacked(both, 1, second)
            wide = jnp.dot(left_h[top:], both[...], preferred_element_type=F32)
            wide = wide + jnp.dot(left_l[top:], both[...], preferred_element_type=F32)
            first, second = wide[:, :width], wide[:, width:]
            first, second = first + swapped(first), second + swapped(second)
            scatter(stage, jnp.where(left_lanes(first), first, second))

        def add_up(stage):
            @pl.when(owns)
            def _():
                block = parts[owner, rows_of(stage)]
                for d in range(1, n):
                    source = (me + d) % n
                    r_copy(stage, owner, source).wait_recv()
                    block = block + in_r[source, rows_of(stage)]
                in_g[owner, rows_of(stage)] = block
                for d in range(1, n):
                    g_copy(stage, owner, d).start()

        def collected(stage):
            for source in range(owners):

                @pl.when(me != first_owner + source)
                def _():
                    g_copy(stage, source, 1).wait_recv()

            return in_g[:, rows_of(stage)].reshape(owners * sizes[stage], width)

        def columns_of(source):
            return pl.ds(pl.multiple_of(source * width, width), width)

        def t_copy(index):
            return pltpu.make_async_remote_copy(
                src_ref=out_t.at[index // 2],
                dst_ref=in_t.at[index],
                send_sem=ts_sem.at[index],
                recv_sem=tr_sem.at[index],
                device_id={"vec": (far, cross, near)[index]},
            )

        def turned(value):
            return jnp.concatenate([value, value], 0).T

        def put_upper(block, one, first, other, second):
            upper = block[:mid]
            left = left_lanes(upper)
            g_ref[:mid, columns_of(one)] = jnp.where(left, upper, first[:mid])
            g_ref[:mid, columns_of(other)] = jnp.where(left, swapped(upper), second[mid:])

        def put_lower(block, last, one, other):
            lower = block[mid:]
            left = left_lanes(lower)
            g_ref[mid:, columns_of(one)] = jnp.where(left, lower, swapped(last))
            g_ref[mid:, columns_of(other)] = jnp.where(left, swapped(lower), last)

        f_copy(0, 0).wait_recv()
        f_copy(2, 0).start()
        f_copy(2, 0).wait_recv()
        multiply(2, 0, in_f[0, 0], in_f[2, 0])
        f_copy(1, 0).wait_recv()
        multiply(0, 0, xs[3, 0], in_f[1, 0])
        f_copy(1, 1).wait_recv()
        multiply(1, mid, xs[3, 1], in_f[1, 1])
        f_copy(0, 1).wait_recv()
        f_copy(2, 1).start()
        f_copy(2, 1).wait_recv()
        multiply(3, mid, in_f[0, 1], in_f[2, 1])
        for stage in (2, 0, 1, 3):
            add_up(stage)
        block = collected(2)
        out_t[0] = block[mid:]
        t_copy(0).start()
        t_copy(1).start()
        mine_block = collected(0)
        out_t[1] = mine_block[mid:]
        t_copy(2).start()
        mine_turned = turned(mine_block[mid:])
        put_lower(mine_block, collected(1), mine, near)
        t_copy(2).wait_recv()
        put_upper(mine_block, mine, mine_turned, near, turned(in_t[2]))
        t_copy(0).wait_recv()
        t_copy(1).wait_recv()
        put_upper(block, far, turned(in_t[0]), cross, turned(in_t[1]))
        put_lower(block, collected(3), far, cross)
        for index in range(3):
            t_copy(index).wait_send()
        for index in range(3):
            for part in range(2):
                f_copy(index, part).wait_send()
        for stage in range(4):
            for target in range(owners):

                @pl.when(me != first_owner + target)
                def _():
                    r_copy(stage, target, me).wait_send()

        @pl.when(owns)
        def _():
            for stage in range(4):
                for d in range(1, n):
                    g_copy(stage, owner, d).wait_send()

    for d in range(1, REACH + 1):

        @pl.when(me >= d)
        def _():
            for step in range(3):
                for part in range(2):
                    x_copy(step, part, d).wait_send()

        @pl.when(me + d < n)
        def _():
            for step in range(3):
                for part in range(2):
                    b_copy(step, part, d).wait_send()


def shards(vectors, hamiltonian, tile_pairs, tile_counts):
    n = lax.axis_size("domain")
    m = lax.axis_size("vec")
    rows, width = vectors.shape
    groups = rows // TILE
    half = rows // 2
    slots = tile_pairs.shape[0]
    lanes = -(-max(slots, (REACH + 1) * groups * groups) // 128) * 128
    with_gram = m == 4 and n % 4 == 0 and width % (8 * n) == 0
    dma = pltpu.SemaphoreType.DMA
    out_shape = [jax.ShapeDtypeStruct((rows, width), F32)]
    scratch = [
        pltpu.VMEM(hamiltonian.shape, F32),
        pltpu.VMEM((rows, width), F32),
        pltpu.VMEM((2, slots), jnp.int32),
        pltpu.VMEM((2, lanes), jnp.int32),
        pltpu.SMEM((2, lanes), jnp.int32),
        pltpu.VMEM((REACH + 1, rows, rows), BF16),
        pltpu.VMEM((REACH + 1, rows, rows), BF16),
        pltpu.VMEM((REACH, rows, rows), BF16),
        pltpu.VMEM((REACH, rows, rows), BF16),
        pltpu.VMEM((rows, 2 * width), BF16),
        pltpu.VMEM((rows, width), BF16),
        pltpu.VMEM((2, half, width), F32),
        pltpu.VMEM((4, 2, half, width), F32),
        pltpu.VMEM((3, 2, REACH, half, width), F32),
        pltpu.VMEM((3, 2, REACH, half, width), F32),
        pltpu.VMEM((3, 2, REACH, half, width), F32),
        dma((4,)),
        dma((3, 2, REACH)),
        dma((3, 2, REACH)),
        dma((3, 2, REACH)),
        dma((3, 2, REACH)),
    ]
    if with_gram:
        out_shape.append(jax.ShapeDtypeStruct((width, m * width), F32))
        scratch += [
            pltpu.VMEM((3, 2, half, width), F32),
            pltpu.VMEM((n // 2, 6 * width // n, width), F32),
            pltpu.VMEM((n, 6 * width // n, width), F32),
            pltpu.VMEM((n // 2, 6 * width // n, width), F32),
            pltpu.VMEM((2, width // 2, width), F32),
            pltpu.VMEM((3, width // 2, width), F32),
            dma((3, 2)),
            dma((3, 2)),
            dma((4, n // 2)),
            dma((4, n)),
            dma((4, n)),
            dma((4, n // 2)),
            dma((3,)),
            dma((3,)),
        ]
    outs = pl.pallas_call(
        functools.partial(filter_kernel, n, m, with_gram),
        out_shape=out_shape,
        in_specs=[
            pl.BlockSpec(memory_space=pltpu.HBM),
            pl.BlockSpec(memory_space=pltpu.HBM),
            pl.BlockSpec(memory_space=pltpu.SMEM),
            pl.BlockSpec(memory_space=pltpu.HBM),
        ],
        out_specs=[pl.BlockSpec(memory_space=pltpu.VMEM)] * len(out_shape),
        scratch_shapes=scratch,
        compiler_params=pltpu.CompilerParams(
            collective_id=0, has_side_effects=True, vmem_limit_bytes=52 * 2**20
        ),
        name="chebyshev",
    )(pltpu.with_memory_space_constraint(vectors, pltpu.HBM), pltpu.with_memory_space_constraint(tile_pairs.T, pltpu.HBM), tile_counts, hamiltonian)
    if with_gram:
        return tuple(outs)
    (filtered,) = outs
    gathered = lax.all_gather(filtered, "vec", axis=1, tiled=True)
    partial_block = jnp.dot(
        filtered.T, gathered, precision=lax.Precision.HIGHEST, preferred_element_type=F32
    ) / (rows * n)
    return (filtered, lax.psum(partial_block, "domain"))


def solution(mesh):
    in_specs = (P("domain", "vec"), P("domain", None, None), P("domain", None), P("domain"))
    out_specs = (P("domain", "vec"), P("vec", None))
    return jax.shard_map(shards, mesh=mesh, in_specs=in_specs, out_specs=out_specs, check_vma=False)
```

```python
import functools

import jax
import jax.numpy as jnp
from jax import lax
from jax.experimental import pallas as pl
from jax.experimental.pallas import tpu as pltpu
from jax.sharding import PartitionSpec as P

TILE = 128
REACH = 2

center_shift = 1.0
half_width = 1.5

F32 = jnp.float32
BF16 = jnp.bfloat16


def halves(value):
    high = value.astype(BF16)
    low = (value - high.astype(F32)).astype(BF16)
    return high, low


def stacked(value):
    return jnp.concatenate(halves(value), 1)


def left_lanes(value):
    return lax.broadcasted_iota(jnp.int32, value.shape, 1) < value.shape[1] // 2


def swapped(value):
    return pltpu.roll(value, value.shape[1] // 2, 1)


def packed(value):
    upper, lower = value[: value.shape[0] // 2], value[value.shape[0] // 2 :]
    left = left_lanes(upper)
    return jnp.where(left, upper, swapped(lower)), jnp.where(left, swapped(upper), lower)


def unpacked(first, second):
    left = left_lanes(first)
    return jnp.where(left, first, swapped(second)), jnp.where(left, swapped(first), second)


def product(high, low, both):
    wide = jnp.dot(high, both, preferred_element_type=F32)
    wide = wide + jnp.dot(low, both, preferred_element_type=F32)
    width = both.shape[1] // 2
    return wide[:, :width] + wide[:, width:]


def packed_product(high, low, both):
    wide = jnp.dot(high, both, preferred_element_type=F32)
    wide = wide + jnp.dot(low, both, preferred_element_type=F32)
    wide = wide + swapped(wide)
    half = wide.shape[0] // 2
    return jnp.where(left_lanes(wide[:half]), wide[:half], wide[half:])


def put_stacked(both, at, value):
    high = value.astype(BF16).astype(F32)
    low = value - high
    left = left_lanes(value)
    half, width = value.shape
    columns = pl.ds(at * width, width)
    both[:half, columns] = jnp.where(left, high, swapped(low)).astype(BF16)
    both[half:, columns] = jnp.where(left, swapped(high), low).astype(BF16)


def put_index(groups, me, pairs, count, index_ref):
    slots = pairs.shape[1]
    span = (REACH + 1) * groups
    lanes = index_ref.shape[1]
    code = (pairs[0:1] - me * groups) * span + pairs[1:2] - me * groups
    row = lax.broadcasted_iota(jnp.int32, (slots, slots), 0)
    lane = lax.broadcasted_iota(jnp.int32, (slots, slots), 1)
    down = jnp.sum(jnp.where(row == lane, code, 0), axis=1, keepdims=True)
    same = (down == code) & (row < lane) & (lane < count)
    index_ref[0:1, :slots] = jnp.max(jnp.where(same, row, -1), axis=0, keepdims=True)
    row = lax.broadcasted_iota(jnp.int32, (slots, lanes), 0)
    lane = lax.broadcasted_iota(jnp.int32, (slots, lanes), 1)
    here = (down == lane) & (row < count)
    index_ref[1:2] = jnp.max(jnp.where(here, row, -1), axis=0, keepdims=True)


def filter_kernel(n, m, with_gram, x_ref, pairs_ref, count_ref, ham_ref, *refs):
    if with_gram:
        f_ref, g_ref, *refs = refs
    else:
        f_ref, *refs = refs
    (tiles, x0, pairs, index_v, index_s, fwd_h, fwd_l, back_h, back_l, both, both_half) = refs[:11]
    (acc, xs, in_x, in_b, out_b) = refs[11:16]
    (load_sem, xs_sem, xr_sem, bs_sem, br_sem) = refs[16:21]
    me = lax.axis_index("domain")
    mine = lax.axis_index("vec")
    rows, width = x_ref.shape
    half = rows // 2
    groups = rows // TILE
    span = (REACH + 1) * groups

    load_pairs = pltpu.make_async_copy(pairs_ref, pairs, load_sem.at[0])
    load_pairs.start()
    load_x = pltpu.make_async_copy(x_ref, x0, load_sem.at[1])
    load_x.start()
    load_tiles = pltpu.make_async_copy(ham_ref, tiles, load_sem.at[2])
    load_tiles.start()

    barrier = pltpu.get_barrier_semaphore()
    if with_gram:
        for d in range(1, n):
            pl.semaphore_signal(barrier, inc=1, device_id={"domain": (me + d) % n})
        for d in range(1, m):
            pl.semaphore_signal(barrier, inc=1, device_id={"vec": (mine + d) % m})
    else:
        for d in range(1, REACH + 1):

            @pl.when(me >= d)
            def _():
                pl.semaphore_signal(barrier, inc=1, device_id={"domain": me - d})

            @pl.when(me + d < n)
            def _():
                pl.semaphore_signal(barrier, inc=1, device_id={"domain": me + d})

    load_pairs.wait()
    put_index(groups, me, pairs[...], count_ref[0], index_v)
    load_index = pltpu.make_async_copy(index_v, index_s, load_sem.at[3])
    load_index.start()

    def rows_at(group):
        return pl.ds(group * TILE, TILE)

    def x_copy(step, part, d):
        return pltpu.make_async_remote_copy(
            src_ref=xs.at[step, part],
            dst_ref=in_x.at[step, part, d - 1],
            send_sem=xs_sem.at[step, part, d - 1],
            recv_sem=xr_sem.at[step, part, d - 1],
            device_id={"domain": me - d},
        )

    def b_copy(step, part, d):
        return pltpu.make_async_remote_copy(
            src_ref=out_b.at[step, part, d - 1],
            dst_ref=in_b.at[step, part, d - 1],
            send_sem=bs_sem.at[step, part, d - 1],
            recv_sem=br_sem.at[step, part, d - 1],
            device_id={"domain": me + d},
        )

    if with_gram:
        (in_f, parts, in_r, in_g, out_t, in_t) = refs[21:27]
        (fs_sem, fr_sem, rs_sem, rr_sem, gs_sem, gr_sem, ts_sem, tr_sem) = refs[27:]
        far = (mine + 2) % 4
        near = mine + 1 - 2 * (mine % 2)
        cross = (near + 2) % 4

        def f_copy(index, part):
            return pltpu.make_async_remote_copy(
                src_ref=in_f.at[0, part] if index == 2 else xs.at[3, part],
                dst_ref=in_f.at[index, part],
                send_sem=fs_sem.at[index, part],
                recv_sem=fr_sem.at[index, part],
                device_id={"vec": far if index == 0 else near},
            )

    load_x.wait()
    both[...] = stacked(x0[...])
    xs[0, 0], xs[0, 1] = packed(x0[...])
    if with_gram:
        pl.semaphore_wait(barrier, n - 1 + m - 1)
    else:
        for d in range(1, REACH + 1):

            @pl.when(me >= d)
            def _():
                pl.semaphore_wait(barrier, 1)

            @pl.when(me + d < n)
            def _():
                pl.semaphore_wait(barrier, 1)

    def send_x(step, part):
        for d in range(1, REACH + 1):

            @pl.when(me >= d)
            def _():
                x_copy(step, part, d).start()

    send_x(0, 0)

    load_index.wait()
    load_tiles.wait()

    def add_before(slot, carry):
        before = index_s[0, slot]
        weight = (before >= 0).astype(F32)
        tiles[slot] = tiles[slot] + tiles[jnp.maximum(before, 0)] * weight
        return carry

    lax.fori_loop(0, tiles.shape[0], add_before, 0, unroll=4)

    def block_at(row, col):
        slot = index_s[1, row * span + col]
        return tiles[jnp.maximum(slot, 0)] * (slot >= 0).astype(F32)

    def put(high, low, index, row, col, value):
        high[index, rows_at(row), rows_at(col)], low[index, rows_at(row), rows_at(col)] = halves(value)

    for d in range(1, REACH + 1):
        for row in range(groups):
            for col in range(groups):
                block = block_at(row, d * groups + col)
                put(fwd_h, fwd_l, d, row, col, block)
                put(back_h, back_l, d - 1, col, row, block.T)

        @pl.when(me + d < n)
        def _():
            first, second = packed(product(back_h[d - 1], back_l[d - 1], both[...]))
            out_b[0, 0, d - 1] = first
            out_b[0, 1, d - 1] = second
            b_copy(0, 0, d).start()

    send_x(0, 1)
    for d in range(1, REACH + 1):

        @pl.when(me + d < n)
        def _():
            b_copy(0, 1, d).start()

    for row in range(groups):
        for col in range(row, groups):
            block = block_at(row, col)
            if row == col:
                put(fwd_h, fwd_l, 0, row, col, 0.5 * (block + block.T))
            else:
                put(fwd_h, fwd_l, 0, row, col, block)
                put(fwd_h, fwd_l, 0, col, row, block.T)

    acc[0], acc[1] = packed(product(fwd_h[0], fwd_l[0], both[...]))
    def add_back(step, part):
        for d in range(1, REACH + 1):

            @pl.when(me >= d)
            def _():
                b_copy(step, part, d).wait_recv()
                acc[part] += in_b[step, part, d - 1]

    def start_step(step, part):
        send_x(step, part)
        put_stacked(both_half, 0, xs[step, part])
        for d in range(1, REACH + 1):

            @pl.when(me + d < n)
            def _():
                out_b[step, part, d - 1] = packed_product(back_h[d - 1], back_l[d - 1], both_half[...])
                b_copy(step, part, d).start()

        acc[part] = packed_product(fwd_h[0], fwd_l[0], both_half[...])

    def one_turn(turn, carry):
        step, part = turn // 2, turn % 2
        for d in range(1, REACH + 1):

            @pl.when(me + d < n)
            def _():
                x_copy(step, part, d).wait_recv()
                put_stacked(both_half, 0, in_x[step, part, d - 1])
                acc[part] += packed_product(fwd_h[d], fwd_l[d], both_half[...])

        add_back(step, part)
        later = (step > 0).astype(F32)
        change = (1.0 + later) * (acc[part] - center_shift * xs[step, part]) / half_width
        xs[step + 1, part] = change - later * xs[jnp.maximum(step - 1, 0), part]

        @pl.when(turn < 4)
        def _():
            start_step(step + 1, part)

        if with_gram:

            @pl.when(turn >= 4)
            def _():
                f_copy(1, part).start()
                f_copy(0, part).start()

        return carry

    lax.fori_loop(0, 6, one_turn, 0)
    f_ref[:half], f_ref[half:] = unpacked(xs[3, 0], xs[3, 1])

    if with_gram:
        left_h, left_l = back_h.at[0, :width], back_l.at[0, :width]
        left_h[...], left_l[...] = halves(f_ref[...].T)
        total = rows * n
        owners, first_owner = n // 2, n // 4
        owner = jnp.clip(me - first_owner, 0, owners - 1)
        owns = (me >= first_owner) & (me < first_owner + owners)
        sizes = [width // owners, width // n] * 2
        mid = width // 2

        def rows_of(stage):
            return pl.ds(sum(sizes[:stage]), sizes[stage])

        def r_copy(stage, target, source):
            return pltpu.make_async_remote_copy(
                src_ref=parts.at[target, rows_of(stage)],
                dst_ref=in_r.at[source, rows_of(stage)],
                send_sem=rs_sem.at[stage, target],
                recv_sem=rr_sem.at[stage, source],
                device_id={"domain": first_owner + target},
            )

        def g_copy(stage, source, d):
            return pltpu.make_async_remote_copy(
                src_ref=in_g.at[source, rows_of(stage)],
                dst_ref=in_g.at[source, rows_of(stage)],
                send_sem=gs_sem.at[stage, d],
                recv_sem=gr_sem.at[stage, source],
                device_id={"domain": (me + d) % n},
            )

        def scatter(stage, block):
            parts[:, rows_of(stage)] = (block / total).reshape(owners, sizes[stage], width)
            for turn in range(owners):
                target = (me + turn) % owners

                @pl.when(me != first_owner + target)
                def _():
                    r_copy(stage, target, me).start()

        def multiply(stage, top, first, second):
            put_stacked(both, 0, first)
            put_stacked(both, 1, second)
            wide = jnp.dot(left_h[top:], both[...], preferred_element_type=F32)
            wide = wide + jnp.dot(left_l[top:], both[...], preferred_element_type=F32)
            first, second = wide[:, :width], wide[:, width:]
            first, second = first + swapped(first), second + swapped(second)
            scatter(stage, jnp.where(left_lanes(first), first, second))

        def add_up(stage):
            @pl.when(owns)
            def _():
                block = parts[owner, rows_of(stage)]
                for d in range(1, n):
                    source = (me + d) % n
                    r_copy(stage, owner, source).wait_recv()
                    block = block + in_r[source, rows_of(stage)]
                in_g[owner, rows_of(stage)] = block
                for d in range(1, n):
                    g_copy(stage, owner, d).start()

        def collected(stage):
            for source in range(owners):

                @pl.when(me != first_owner + source)
                def _():
                    g_copy(stage, source, 1).wait_recv()

            return in_g[:, rows_of(stage)].reshape(owners * sizes[stage], width)

        def columns_of(source):
            return pl.ds(pl.multiple_of(source * width, width), width)

        def t_copy(index):
            return pltpu.make_async_remote_copy(
                src_ref=out_t.at[index // 2],
                dst_ref=in_t.at[index],
                send_sem=ts_sem.at[index],
                recv_sem=tr_sem.at[index],
                device_id={"vec": (far, cross, near)[index]},
            )

        def turned(value):
            return jnp.concatenate([value, value], 0).T

        def put_upper(block, one, first, other, second):
            upper = block[:mid]
            left = left_lanes(upper)
            g_ref[:mid, columns_of(one)] = jnp.where(left, upper, first[:mid])
            g_ref[:mid, columns_of(other)] = jnp.where(left, swapped(upper), second[mid:])

        def put_lower(block, last, one, other):
            lower = block[mid:]
            left = left_lanes(lower)
            g_ref[mid:, columns_of(one)] = jnp.where(left, lower, swapped(last))
            g_ref[mid:, columns_of(other)] = jnp.where(left, swapped(lower), last)

        f_copy(0, 0).wait_recv()
        f_copy(2, 0).start()
        f_copy(2, 0).wait_recv()
        multiply(2, 0, in_f[0, 0], in_f[2, 0])
        f_copy(1, 0).wait_recv()
        multiply(0, 0, xs[3, 0], in_f[1, 0])
        f_copy(1, 1).wait_recv()
        multiply(1, mid, xs[3, 1], in_f[1, 1])
        f_copy(0, 1).wait_recv()
        f_copy(2, 1).start()
        f_copy(2, 1).wait_recv()
        multiply(3, mid, in_f[0, 1], in_f[2, 1])
        for stage in (2, 0, 1, 3):
            add_up(stage)
        block = collected(2)
        out_t[0] = block[mid:]
        t_copy(0).start()
        t_copy(1).start()
        mine_block = collected(0)
        out_t[1] = mine_block[mid:]
        t_copy(2).start()
        mine_turned = turned(mine_block[mid:])
        put_lower(mine_block, collected(1), mine, near)
        t_copy(2).wait_recv()
        put_upper(mine_block, mine, mine_turned, near, turned(in_t[2]))
        t_copy(0).wait_recv()
        t_copy(1).wait_recv()
        put_upper(block, far, turned(in_t[0]), cross, turned(in_t[1]))
        put_lower(block, collected(3), far, cross)
        for index in range(3):
            t_copy(index).wait_send()
        for index in range(3):
            for part in range(2):
                f_copy(index, part).wait_send()
        for stage in range(4):
            for target in range(owners):

                @pl.when(me != first_owner + target)
                def _():
                    r_copy(stage, target, me).wait_send()

        @pl.when(owns)
        def _():
            for stage in range(4):
                for d in range(1, n):
                    g_copy(stage, owner, d).wait_send()

    for d in range(1, REACH + 1):

        @pl.when(me >= d)
        def _():
            for step in range(3):
                for part in range(2):
                    x_copy(step, part, d).wait_send()

        @pl.when(me + d < n)
        def _():
            for step in range(3):
                for part in range(2):
                    b_copy(step, part, d).wait_send()


def shards(vectors, hamiltonian, tile_pairs, tile_counts):
    n = lax.axis_size("domain")
    m = lax.axis_size("vec")
    rows, width = vectors.shape
    groups = rows // TILE
    half = rows // 2
    slots = tile_pairs.shape[0]
    lanes = -(-max(slots, (REACH + 1) * groups * groups) // 128) * 128
    with_gram = m == 4 and n % 4 == 0 and width % (8 * n) == 0
    dma = pltpu.SemaphoreType.DMA
    out_shape = [jax.ShapeDtypeStruct((rows, width), F32)]
    scratch = [
        pltpu.VMEM(hamiltonian.shape, F32),
        pltpu.VMEM((rows, width), F32),
        pltpu.VMEM((2, slots), jnp.int32),
        pltpu.VMEM((2, lanes), jnp.int32),
        pltpu.SMEM((2, lanes), jnp.int32),
        pltpu.VMEM((REACH + 1, rows, rows), BF16),
        pltpu.VMEM((REACH + 1, rows, rows), BF16),
        pltpu.VMEM((REACH, rows, rows), BF16),
        pltpu.VMEM((REACH, rows, rows), BF16),
        pltpu.VMEM((rows, 2 * width), BF16),
        pltpu.VMEM((rows, width), BF16),
        pltpu.VMEM((2, half, width), F32),
        pltpu.VMEM((4, 2, half, width), F32),
        pltpu.VMEM((3, 2, REACH, half, width), F32),
        pltpu.VMEM((3, 2, REACH, half, width), F32),
        pltpu.VMEM((3, 2, REACH, half, width), F32),
        dma((4,)),
        dma((3, 2, REACH)),
        dma((3, 2, REACH)),
        dma((3, 2, REACH)),
        dma((3, 2, REACH)),
    ]
    if with_gram:
        out_shape.append(jax.ShapeDtypeStruct((width, m * width), F32))
        scratch += [
            pltpu.VMEM((3, 2, half, width), F32),
            pltpu.VMEM((n // 2, 6 * width // n, width), F32),
            pltpu.VMEM((n, 6 * width // n, width), F32),
            pltpu.VMEM((n // 2, 6 * width // n, width), F32),
            pltpu.VMEM((2, width // 2, width), F32),
            pltpu.VMEM((3, width // 2, width), F32),
            dma((3, 2)),
            dma((3, 2)),
            dma((4, n // 2)),
            dma((4, n)),
            dma((4, n)),
            dma((4, n // 2)),
            dma((3,)),
            dma((3,)),
        ]
    outs = pl.pallas_call(
        functools.partial(filter_kernel, n, m, with_gram),
        out_shape=out_shape,
        in_specs=[
            pl.BlockSpec(memory_space=pltpu.HBM),
            pl.BlockSpec(memory_space=pltpu.HBM),
            pl.BlockSpec(memory_space=pltpu.SMEM),
            pl.BlockSpec(memory_space=pltpu.HBM),
        ],
        out_specs=[pl.BlockSpec(memory_space=pltpu.VMEM)] * len(out_shape),
        scratch_shapes=scratch,
        compiler_params=pltpu.CompilerParams(
            collective_id=0, has_side_effects=True, vmem_limit_bytes=52 * 2**20
        ),
        name="chebyshev",
    )(pltpu.with_memory_space_constraint(vectors, pltpu.HBM), pltpu.with_memory_space_constraint(tile_pairs.T, pltpu.HBM), tile_counts, hamiltonian)
    if with_gram:
        return tuple(outs)
    (filtered,) = outs
    gathered = lax.all_gather(filtered, "vec", axis=1, tiled=True)
    partial_block = jnp.dot(
        filtered.T, gathered, precision=lax.Precision.HIGHEST, preferred_element_type=F32
    ) / (rows * n)
    return (filtered, lax.psum(partial_block, "domain"))


def solution(mesh):
    in_specs = (P("domain", "vec"), P("domain", None, None), P("domain", None), P("domain"))
    out_specs = (P("domain", "vec"), P("vec", None))
    return jax.shard_map(shards, mesh=mesh, in_specs=in_specs, out_specs=out_specs, check_vma=False)
```

```python
import functools

import jax
import jax.numpy as jnp
from jax import lax
from jax.experimental import pallas as pl
from jax.experimental.pallas import tpu as pltpu
from jax.sharding import PartitionSpec as P

TILE = 128
REACH = 2

center_shift = 1.0
half_width = 1.5

F32 = jnp.float32
BF16 = jnp.bfloat16


def halves(value):
    high = value.astype(BF16)
    low = (value - high.astype(F32)).astype(BF16)
    return high, low


def stacked(value):
    return jnp.concatenate(halves(value), 1)


def left_lanes(value):
    return lax.broadcasted_iota(jnp.int32, value.shape, 1) < value.shape[1] // 2


def swapped(value):
    return pltpu.roll(value, value.shape[1] // 2, 1)


def packed(value):
    upper, lower = value[: value.shape[0] // 2], value[value.shape[0] // 2 :]
    left = left_lanes(upper)
    return jnp.where(left, upper, swapped(lower)), jnp.where(left, swapped(upper), lower)


def unpacked(first, second):
    left = left_lanes(first)
    return jnp.where(left, first, swapped(second)), jnp.where(left, swapped(first), second)


def product(high, low, both):
    wide = jnp.dot(high, both, preferred_element_type=F32)
    wide = wide + jnp.dot(low, both, preferred_element_type=F32)
    width = both.shape[1] // 2
    return wide[:, :width] + wide[:, width:]


def packed_product(high, low, both):
    wide = jnp.dot(high, both, preferred_element_type=F32)
    wide = wide + jnp.dot(low, both, preferred_element_type=F32)
    wide = wide + swapped(wide)
    half = wide.shape[0] // 2
    return jnp.where(left_lanes(wide[:half]), wide[:half], wide[half:])


def put_stacked(both, at, value):
    high = value.astype(BF16).astype(F32)
    low = value - high
    left = left_lanes(value)
    half, width = value.shape
    columns = pl.ds(at * width, width)
    both[:half, columns] = jnp.where(left, high, swapped(low)).astype(BF16)
    both[half:, columns] = jnp.where(left, swapped(high), low).astype(BF16)


def put_index(groups, me, pairs, count, index_ref):
    slots = pairs.shape[1]
    span = (REACH + 1) * groups
    lanes = index_ref.shape[1]
    code = (pairs[0:1] - me * groups) * span + pairs[1:2] - me * groups
    row = lax.broadcasted_iota(jnp.int32, (slots, slots), 0)
    lane = lax.broadcasted_iota(jnp.int32, (slots, slots), 1)
    down = jnp.sum(jnp.where(row == lane, code, 0), axis=1, keepdims=True)
    same = (down == code) & (row < lane) & (lane < count)
    index_ref[0:1, :slots] = jnp.max(jnp.where(same, row, -1), axis=0, keepdims=True)
    row = lax.broadcasted_iota(jnp.int32, (slots, lanes), 0)
    lane = lax.broadcasted_iota(jnp.int32, (slots, lanes), 1)
    here = (down == lane) & (row < count)
    index_ref[1:2] = jnp.max(jnp.where(here, row, -1), axis=0, keepdims=True)


def filter_kernel(n, m, with_gram, x_ref, pairs_ref, count_ref, ham_ref, *refs):
    if with_gram:
        f_ref, g_ref, *refs = refs
    else:
        f_ref, *refs = refs
    (tiles, x0, pairs, index_v, index_s, fwd_h, fwd_l, back_h, back_l, both, both_half) = refs[:11]
    (acc, xs, in_x, in_b, out_b) = refs[11:16]
    (load_sem, xs_sem, xr_sem, bs_sem, br_sem) = refs[16:21]
    me = lax.axis_index("domain")
    mine = lax.axis_index("vec")
    rows, width = x_ref.shape
    half = rows // 2
    groups = rows // TILE
    span = (REACH + 1) * groups

    load_pairs = pltpu.make_async_copy(pairs_ref, pairs, load_sem.at[0])
    load_pairs.start()
    load_x = pltpu.make_async_copy(x_ref, x0, load_sem.at[1])
    load_x.start()
    load_tiles = pltpu.make_async_copy(ham_ref, tiles, load_sem.at[2])
    load_tiles.start()

    barrier = pltpu.get_barrier_semaphore()
    if with_gram:
        for d in range(1, n):
            pl.semaphore_signal(barrier, inc=1, device_id={"domain": (me + d) % n})
        for d in range(1, m):
            pl.semaphore_signal(barrier, inc=1, device_id={"vec": (mine + d) % m})
    else:
        for d in range(1, REACH + 1):

            @pl.when(me >= d)
            def _():
                pl.semaphore_signal(barrier, inc=1, device_id={"domain": me - d})

            @pl.when(me + d < n)
            def _():
                pl.semaphore_signal(barrier, inc=1, device_id={"domain": me + d})

    load_pairs.wait()
    put_index(groups, me, pairs[...], count_ref[0], index_v)
    load_index = pltpu.make_async_copy(index_v, index_s, load_sem.at[3])
    load_index.start()

    def rows_at(group):
        return pl.ds(group * TILE, TILE)

    def x_copy(step, part, d):
        return pltpu.make_async_remote_copy(
            src_ref=xs.at[step, part],
            dst_ref=in_x.at[step, part, d - 1],
            send_sem=xs_sem.at[step, part, d - 1],
            recv_sem=xr_sem.at[step, part, d - 1],
            device_id={"domain": me - d},
        )

    def b_copy(step, part, d):
        return pltpu.make_async_remote_copy(
            src_ref=out_b.at[step, part, d - 1],
            dst_ref=in_b.at[step, part, d - 1],
            send_sem=bs_sem.at[step, part, d - 1],
            recv_sem=br_sem.at[step, part, d - 1],
            device_id={"domain": me + d},
        )

    if with_gram:
        (in_f, parts, in_r, in_g, out_t, in_t) = refs[21:27]
        (fs_sem, fr_sem, rs_sem, rr_sem, gs_sem, gr_sem, ts_sem, tr_sem) = refs[27:]
        far = (mine + 2) % 4
        near = mine + 1 - 2 * (mine % 2)
        cross = (near + 2) % 4

        def f_copy(index, part):
            return pltpu.make_async_remote_copy(
                src_ref=in_f.at[0, part] if index == 2 else xs.at[3, part],
                dst_ref=in_f.at[index, part],
                send_sem=fs_sem.at[index, part],
                recv_sem=fr_sem.at[index, part],
                device_id={"vec": far if index == 0 else near},
            )

    load_x.wait()
    both[...] = stacked(x0[...])
    xs[0, 0], xs[0, 1] = packed(x0[...])
    if with_gram:
        pl.semaphore_wait(barrier, n - 1 + m - 1)
    else:
        for d in range(1, REACH + 1):

            @pl.when(me >= d)
            def _():
                pl.semaphore_wait(barrier, 1)

            @pl.when(me + d < n)
            def _():
                pl.semaphore_wait(barrier, 1)

    def send_x(step, part):
        for d in range(1, REACH + 1):

            @pl.when(me >= d)
            def _():
                x_copy(step, part, d).start()

    send_x(0, 0)

    load_index.wait()
    load_tiles.wait()

    def add_before(slot, carry):
        before = index_s[0, slot]
        weight = (before >= 0).astype(F32)
        tiles[slot] = tiles[slot] + tiles[jnp.maximum(before, 0)] * weight
        return carry

    lax.fori_loop(0, tiles.shape[0], add_before, 0, unroll=4)

    def block_at(row, col):
        slot = index_s[1, row * span + col]
        return tiles[jnp.maximum(slot, 0)] * (slot >= 0).astype(F32)

    def put(high, low, index, row, col, value):
        high[index, rows_at(row), rows_at(col)], low[index, rows_at(row), rows_at(col)] = halves(value)

    for d in range(1, REACH + 1):
        for row in range(groups):
            for col in range(groups):
                block = block_at(row, d * groups + col)
                put(fwd_h, fwd_l, d, row, col, block)
                put(back_h, back_l, d - 1, col, row, block.T)

        @pl.when(me + d < n)
        def _():
            first, second = packed(product(back_h[d - 1], back_l[d - 1], both[...]))
            out_b[0, 0, d - 1] = first
            out_b[0, 1, d - 1] = second
            b_copy(0, 0, d).start()

    send_x(0, 1)
    for d in range(1, REACH + 1):

        @pl.when(me + d < n)
        def _():
            b_copy(0, 1, d).start()

    for row in range(groups):
        for col in range(row, groups):
            block = block_at(row, col)
            if row == col:
                put(fwd_h, fwd_l, 0, row, col, 0.5 * (block + block.T))
            else:
                put(fwd_h, fwd_l, 0, row, col, block)
                put(fwd_h, fwd_l, 0, col, row, block.T)

    acc[0], acc[1] = packed(product(fwd_h[0], fwd_l[0], both[...]))
    def add_back(step, part):
        for d in range(1, REACH + 1):

            @pl.when(me >= d)
            def _():
                b_copy(step, part, d).wait_recv()
                acc[part] += in_b[step, part, d - 1]

    def start_step(step, part):
        send_x(step, part)
        put_stacked(both_half, 0, xs[step, part])
        for d in range(1, REACH + 1):

            @pl.when(me + d < n)
            def _():
                out_b[step, part, d - 1] = packed_product(back_h[d - 1], back_l[d - 1], both_half[...])
                b_copy(step, part, d).start()

        acc[part] = packed_product(fwd_h[0], fwd_l[0], both_half[...])

    def one_turn(turn, carry):
        step, part = turn // 2, turn % 2
        for d in range(1, REACH + 1):

            @pl.when(me + d < n)
            def _():
                x_copy(step, part, d).wait_recv()
                put_stacked(both_half, 0, in_x[step, part, d - 1])
                acc[part] += packed_product(fwd_h[d], fwd_l[d], both_half[...])

        add_back(step, part)
        later = (step > 0).astype(F32)
        change = (1.0 + later) * (acc[part] - center_shift * xs[step, part]) * (1.0 / half_width)
        xs[step + 1, part] = change - later * xs[jnp.maximum(step - 1, 0), part]

        @pl.when(turn < 4)
        def _():
            start_step(step + 1, part)

        if with_gram:

            @pl.when(turn >= 4)
            def _():
                f_copy(1, part).start()
                f_copy(0, part).start()

        return carry

    lax.fori_loop(0, 6, one_turn, 0)
    f_ref[:half], f_ref[half:] = unpacked(xs[3, 0], xs[3, 1])

    if with_gram:
        left_h, left_l = back_h.at[0, :width], back_l.at[0, :width]
        left_h[...], left_l[...] = halves(f_ref[...].T)
        total = rows * n
        owners, first_owner = n // 2, n // 4
        owner = jnp.clip(me - first_owner, 0, owners - 1)
        owns = (me >= first_owner) & (me < first_owner + owners)
        sizes = [width // owners, width // n] * 2
        mid = width // 2

        def rows_of(stage):
            return pl.ds(sum(sizes[:stage]), sizes[stage])

        def r_copy(stage, target, source):
            return pltpu.make_async_remote_copy(
                src_ref=parts.at[target, rows_of(stage)],
                dst_ref=in_r.at[source, rows_of(stage)],
                send_sem=rs_sem.at[stage, target],
                recv_sem=rr_sem.at[stage, source],
                device_id={"domain": first_owner + target},
            )

        def g_copy(stage, source, d):
            return pltpu.make_async_remote_copy(
                src_ref=in_g.at[source, rows_of(stage)],
                dst_ref=in_g.at[source, rows_of(stage)],
                send_sem=gs_sem.at[stage, d],
                recv_sem=gr_sem.at[stage, source],
                device_id={"domain": (me + d) % n},
            )

        def scatter(stage, block):
            parts[:, rows_of(stage)] = (block / total).reshape(owners, sizes[stage], width)
            for turn in range(owners):
                target = (me + turn) % owners

                @pl.when(me != first_owner + target)
                def _():
                    r_copy(stage, target, me).start()

        def multiply(stage, top, first, second):
            put_stacked(both, 0, first)
            put_stacked(both, 1, second)
            wide = jnp.dot(left_h[top:], both[...], preferred_element_type=F32)
            wide = wide + jnp.dot(left_l[top:], both[...], preferred_element_type=F32)
            first, second = wide[:, :width], wide[:, width:]
            first, second = first + swapped(first), second + swapped(second)
            scatter(stage, jnp.where(left_lanes(first), first, second))

        def add_up(stage):
            @pl.when(owns)
            def _():
                block = parts[owner, rows_of(stage)]
                for d in range(1, n):
                    source = (me + d) % n
                    r_copy(stage, owner, source).wait_recv()
                    block = block + in_r[source, rows_of(stage)]
                in_g[owner, rows_of(stage)] = block
                for d in range(1, n):
                    g_copy(stage, owner, d).start()

        def collected(stage):
            for source in range(owners):

                @pl.when(me != first_owner + source)
                def _():
                    g_copy(stage, source, 1).wait_recv()

            return in_g[:, rows_of(stage)].reshape(owners * sizes[stage], width)

        def columns_of(source):
            return pl.ds(pl.multiple_of(source * width, width), width)

        def t_copy(index):
            return pltpu.make_async_remote_copy(
                src_ref=out_t.at[index // 2],
                dst_ref=in_t.at[index],
                send_sem=ts_sem.at[index],
                recv_sem=tr_sem.at[index],
                device_id={"vec": (far, cross, near)[index]},
            )

        def turned(value):
            return jnp.concatenate([value, value], 0).T

        def put_upper(block, one, first, other, second):
            upper = block[:mid]
            left = left_lanes(upper)
            g_ref[:mid, columns_of(one)] = jnp.where(left, upper, first[:mid])
            g_ref[:mid, columns_of(other)] = jnp.where(left, swapped(upper), second[mid:])

        def put_lower(block, last, one, other):
            lower = block[mid:]
            left = left_lanes(lower)
            g_ref[mid:, columns_of(one)] = jnp.where(left, lower, swapped(last))
            g_ref[mid:, columns_of(other)] = jnp.where(left, swapped(lower), last)

        f_copy(0, 0).wait_recv()
        f_copy(2, 0).start()
        f_copy(2, 0).wait_recv()
        multiply(2, 0, in_f[0, 0], in_f[2, 0])
        f_copy(1, 0).wait_recv()
        multiply(0, 0, xs[3, 0], in_f[1, 0])
        f_copy(1, 1).wait_recv()
        multiply(1, mid, xs[3, 1], in_f[1, 1])
        f_copy(0, 1).wait_recv()
        f_copy(2, 1).start()
        f_copy(2, 1).wait_recv()
        multiply(3, mid, in_f[0, 1], in_f[2, 1])
        for stage in (2, 0, 1, 3):
            add_up(stage)
        block = collected(2)
        out_t[0] = block[mid:]
        t_copy(0).start()
        t_copy(1).start()
        mine_block = collected(0)
        out_t[1] = mine_block[mid:]
        t_copy(2).start()
        mine_turned = turned(mine_block[mid:])
        put_lower(mine_block, collected(1), mine, near)
        t_copy(2).wait_recv()
        put_upper(mine_block, mine, mine_turned, near, turned(in_t[2]))
        t_copy(0).wait_recv()
        t_copy(1).wait_recv()
        put_upper(block, far, turned(in_t[0]), cross, turned(in_t[1]))
        put_lower(block, collected(3), far, cross)
        for index in range(3):
            t_copy(index).wait_send()
        for index in range(3):
            for part in range(2):
                f_copy(index, part).wait_send()
        for stage in range(4):
            for target in range(owners):

                @pl.when(me != first_owner + target)
                def _():
                    r_copy(stage, target, me).wait_send()

        @pl.when(owns)
        def _():
            for stage in range(4):
                for d in range(1, n):
                    g_copy(stage, owner, d).wait_send()

    for d in range(1, REACH + 1):

        @pl.when(me >= d)
        def _():
            for step in range(3):
                for part in range(2):
                    x_copy(step, part, d).wait_send()

        @pl.when(me + d < n)
        def _():
            for step in range(3):
                for part in range(2):
                    b_copy(step, part, d).wait_send()


def shards(vectors, hamiltonian, tile_pairs, tile_counts):
    n = lax.axis_size("domain")
    m = lax.axis_size("vec")
    rows, width = vectors.shape
    groups = rows // TILE
    half = rows // 2
    slots = tile_pairs.shape[0]
    lanes = -(-max(slots, (REACH + 1) * groups * groups) // 128) * 128
    with_gram = m == 4 and n % 4 == 0 and width % (8 * n) == 0
    dma = pltpu.SemaphoreType.DMA
    out_shape = [jax.ShapeDtypeStruct((rows, width), F32)]
    scratch = [
        pltpu.VMEM(hamiltonian.shape, F32),
        pltpu.VMEM((rows, width), F32),
        pltpu.VMEM((2, slots), jnp.int32),
        pltpu.VMEM((2, lanes), jnp.int32),
        pltpu.SMEM((2, lanes), jnp.int32),
        pltpu.VMEM((REACH + 1, rows, rows), BF16),
        pltpu.VMEM((REACH + 1, rows, rows), BF16),
        pltpu.VMEM((REACH, rows, rows), BF16),
        pltpu.VMEM((REACH, rows, rows), BF16),
        pltpu.VMEM((rows, 2 * width), BF16),
        pltpu.VMEM((rows, width), BF16),
        pltpu.VMEM((2, half, width), F32),
        pltpu.VMEM((4, 2, half, width), F32),
        pltpu.VMEM((3, 2, REACH, half, width), F32),
        pltpu.VMEM((3, 2, REACH, half, width), F32),
        pltpu.VMEM((3, 2, REACH, half, width), F32),
        dma((4,)),
        dma((3, 2, REACH)),
        dma((3, 2, REACH)),
        dma((3, 2, REACH)),
        dma((3, 2, REACH)),
    ]
    if with_gram:
        out_shape.append(jax.ShapeDtypeStruct((width, m * width), F32))
        scratch += [
            pltpu.VMEM((3, 2, half, width), F32),
            pltpu.VMEM((n // 2, 6 * width // n, width), F32),
            pltpu.VMEM((n, 6 * width // n, width), F32),
            pltpu.VMEM((n // 2, 6 * width // n, width), F32),
            pltpu.VMEM((2, width // 2, width), F32),
            pltpu.VMEM((3, width // 2, width), F32),
            dma((3, 2)),
            dma((3, 2)),
            dma((4, n // 2)),
            dma((4, n)),
            dma((4, n)),
            dma((4, n // 2)),
            dma((3,)),
            dma((3,)),
        ]
    outs = pl.pallas_call(
        functools.partial(filter_kernel, n, m, with_gram),
        out_shape=out_shape,
        in_specs=[
            pl.BlockSpec(memory_space=pltpu.HBM),
            pl.BlockSpec(memory_space=pltpu.HBM),
            pl.BlockSpec(memory_space=pltpu.SMEM),
            pl.BlockSpec(memory_space=pltpu.HBM),
        ],
        out_specs=[pl.BlockSpec(memory_space=pltpu.VMEM)] * len(out_shape),
        scratch_shapes=scratch,
        compiler_params=pltpu.CompilerParams(
            collective_id=0, has_side_effects=True, vmem_limit_bytes=52 * 2**20
        ),
        name="chebyshev",
    )(pltpu.with_memory_space_constraint(vectors, pltpu.HBM), pltpu.with_memory_space_constraint(tile_pairs.T, pltpu.HBM), tile_counts, hamiltonian)
    if with_gram:
        return tuple(outs)
    (filtered,) = outs
    gathered = lax.all_gather(filtered, "vec", axis=1, tiled=True)
    partial_block = jnp.dot(
        filtered.T, gathered, precision=lax.Precision.HIGHEST, preferred_element_type=F32
    ) / (rows * n)
    return (filtered, lax.psum(partial_block, "domain"))


def solution(mesh):
    in_specs = (P("domain", "vec"), P("domain", None, None), P("domain", None), P("domain"))
    out_specs = (P("domain", "vec"), P("vec", None))
    return jax.shard_map(shards, mesh=mesh, in_specs=in_specs, out_specs=out_specs, check_vma=False)
```

```python
import functools

import jax
import jax.numpy as jnp
from jax import lax
from jax.experimental import pallas as pl
from jax.experimental.pallas import tpu as pltpu
from jax.sharding import PartitionSpec as P

TILE = 128
REACH = 2

center_shift = 1.0
half_width = 1.5

F32 = jnp.float32
BF16 = jnp.bfloat16


def halves(value):
    high = value.astype(BF16)
    low = (value - high.astype(F32)).astype(BF16)
    return high, low


def stacked(value):
    return jnp.concatenate(halves(value), 1)


def left_lanes(value):
    return lax.broadcasted_iota(jnp.int32, value.shape, 1) < value.shape[1] // 2


def swapped(value):
    return pltpu.roll(value, value.shape[1] // 2, 1)


def packed(value):
    upper, lower = value[: value.shape[0] // 2], value[value.shape[0] // 2 :]
    left = left_lanes(upper)
    return jnp.where(left, upper, swapped(lower)), jnp.where(left, swapped(upper), lower)


def unpacked(first, second):
    left = left_lanes(first)
    return jnp.where(left, first, swapped(second)), jnp.where(left, swapped(first), second)


def product(high, low, both):
    wide = jnp.dot(high, both, preferred_element_type=F32)
    wide = wide + jnp.dot(low, both, preferred_element_type=F32)
    width = both.shape[1] // 2
    return wide[:, :width] + wide[:, width:]


def packed_product(high, low, both):
    wide = jnp.dot(high, both, preferred_element_type=F32)
    wide = wide + jnp.dot(low, both, preferred_element_type=F32)
    wide = wide + swapped(wide)
    half = wide.shape[0] // 2
    return jnp.where(left_lanes(wide[:half]), wide[:half], wide[half:])


def put_stacked(both, at, value):
    high = value.astype(BF16).astype(F32)
    low = value - high
    left = left_lanes(value)
    half, width = value.shape
    columns = pl.ds(at * width, width)
    both[:half, columns] = jnp.where(left, high, swapped(low)).astype(BF16)
    both[half:, columns] = jnp.where(left, swapped(high), low).astype(BF16)


def put_index(groups, me, pairs, count, index_ref):
    slots = pairs.shape[1]
    span = (REACH + 1) * groups
    lanes = index_ref.shape[1]
    code = (pairs[0:1] - me * groups) * span + pairs[1:2] - me * groups
    row = lax.broadcasted_iota(jnp.int32, (slots, slots), 0)
    lane = lax.broadcasted_iota(jnp.int32, (slots, slots), 1)
    down = jnp.sum(jnp.where(row == lane, code, 0), axis=1, keepdims=True)
    same = (down == code) & (row < lane) & (lane < count)
    index_ref[0:1, :slots] = jnp.max(jnp.where(same, row, -1), axis=0, keepdims=True)
    row = lax.broadcasted_iota(jnp.int32, (slots, lanes), 0)
    lane = lax.broadcasted_iota(jnp.int32, (slots, lanes), 1)
    here = (down == lane) & (row < count)
    index_ref[1:2] = jnp.max(jnp.where(here, row, -1), axis=0, keepdims=True)


def filter_kernel(n, m, with_gram, x_ref, pairs_ref, count_ref, ham_ref, *refs):
    if with_gram:
        f_ref, g_ref, *refs = refs
    else:
        f_ref, *refs = refs
    (tiles, x0, pairs, index_v, index_s, fwd_h, fwd_l, back_h, back_l, both, both_half) = refs[:11]
    (acc, xs, in_x, in_b, out_b) = refs[11:16]
    (load_sem, xs_sem, xr_sem, bs_sem, br_sem) = refs[16:21]
    me = lax.axis_index("domain")
    mine = lax.axis_index("vec")
    rows, width = x_ref.shape
    half = rows // 2
    groups = rows // TILE
    span = (REACH + 1) * groups

    load_pairs = pltpu.make_async_copy(pairs_ref, pairs, load_sem.at[0])
    load_pairs.start()
    load_x = pltpu.make_async_copy(x_ref, x0, load_sem.at[1])
    load_x.start()
    load_tiles = pltpu.make_async_copy(ham_ref, tiles, load_sem.at[2])
    load_tiles.start()

    barrier = pltpu.get_barrier_semaphore()
    if with_gram:
        for d in range(1, n):
            pl.semaphore_signal(barrier, inc=1, device_id={"domain": (me + d) % n})
        for d in range(1, m):
            pl.semaphore_signal(barrier, inc=1, device_id={"vec": (mine + d) % m})
    else:
        for d in range(1, REACH + 1):

            @pl.when(me >= d)
            def _():
                pl.semaphore_signal(barrier, inc=1, device_id={"domain": me - d})

            @pl.when(me + d < n)
            def _():
                pl.semaphore_signal(barrier, inc=1, device_id={"domain": me + d})

    load_pairs.wait()
    put_index(groups, me, pairs[...], count_ref[0], index_v)
    load_index = pltpu.make_async_copy(index_v, index_s, load_sem.at[3])
    load_index.start()

    def rows_at(group):
        return pl.ds(group * TILE, TILE)

    def x_copy(step, part, d):
        return pltpu.make_async_remote_copy(
            src_ref=xs.at[step, part],
            dst_ref=in_x.at[step, part, d - 1],
            send_sem=xs_sem.at[step, part, d - 1],
            recv_sem=xr_sem.at[step, part, d - 1],
            device_id={"domain": me - d},
        )

    def b_copy(step, part, d):
        return pltpu.make_async_remote_copy(
            src_ref=out_b.at[step, part, d - 1],
            dst_ref=in_b.at[step, part, d - 1],
            send_sem=bs_sem.at[step, part, d - 1],
            recv_sem=br_sem.at[step, part, d - 1],
            device_id={"domain": me + d},
        )

    if with_gram:
        (in_f, parts, in_r, in_g, out_t, in_t) = refs[21:27]
        (fs_sem, fr_sem, rs_sem, rr_sem, gs_sem, gr_sem, ts_sem, tr_sem) = refs[27:]
        far = (mine + 2) % 4
        near = mine + 1 - 2 * (mine % 2)
        cross = (near + 2) % 4

        def f_copy(index, part):
            return pltpu.make_async_remote_copy(
                src_ref=in_f.at[0, part] if index == 2 else xs.at[3, part],
                dst_ref=in_f.at[index, part],
                send_sem=fs_sem.at[index, part],
                recv_sem=fr_sem.at[index, part],
                device_id={"vec": far if index == 0 else near},
            )

    load_x.wait()
    both[...] = stacked(x0[...])
    xs[0, 0], xs[0, 1] = packed(x0[...])
    if with_gram:
        pl.semaphore_wait(barrier, n - 1 + m - 1)
    else:
        for d in range(1, REACH + 1):

            @pl.when(me >= d)
            def _():
                pl.semaphore_wait(barrier, 1)

            @pl.when(me + d < n)
            def _():
                pl.semaphore_wait(barrier, 1)

    def send_x(step, part):
        for d in range(1, REACH + 1):

            @pl.when(me >= d)
            def _():
                x_copy(step, part, d).start()

    send_x(0, 0)

    load_index.wait()
    load_tiles.wait()

    def add_before(slot, carry):
        before = index_s[0, slot]
        weight = (before >= 0).astype(F32)
        tiles[slot] = tiles[slot] + tiles[jnp.maximum(before, 0)] * weight
        return carry

    lax.fori_loop(0, tiles.shape[0], add_before, 0, unroll=4)

    def block_at(row, col):
        slot = index_s[1, row * span + col]
        return tiles[jnp.maximum(slot, 0)] * (slot >= 0).astype(F32)

    def put(high, low, index, row, col, value):
        high[index, rows_at(row), rows_at(col)], low[index, rows_at(row), rows_at(col)] = halves(value)

    for d in range(1, REACH + 1):
        for row in range(groups):
            for col in range(groups):
                block = block_at(row, d * groups + col)
                put(fwd_h, fwd_l, d, row, col, block)
                put(back_h, back_l, d - 1, col, row, block.T)

        @pl.when(me + d < n)
        def _():
            first, second = packed(product(back_h[d - 1], back_l[d - 1], both[...]))
            out_b[0, 0, d - 1] = first
            out_b[0, 1, d - 1] = second
            b_copy(0, 0, d).start()

    send_x(0, 1)
    for d in range(1, REACH + 1):

        @pl.when(me + d < n)
        def _():
            b_copy(0, 1, d).start()

    for row in range(groups):
        for col in range(row, groups):
            block = block_at(row, col)
            if row == col:
                put(fwd_h, fwd_l, 0, row, col, 0.5 * (block + block.T))
            else:
                put(fwd_h, fwd_l, 0, row, col, block)
                put(fwd_h, fwd_l, 0, col, row, block.T)

    acc[0], acc[1] = packed(product(fwd_h[0], fwd_l[0], both[...]))
    def add_back(step, part):
        for d in range(1, REACH + 1):

            @pl.when(me >= d)
            def _():
                b_copy(step, part, d).wait_recv()
                acc[part] += in_b[step, part, d - 1]

    def start_step(step, part):
        send_x(step, part)
        put_stacked(both_half, 0, xs[step, part])
        for d in range(1, REACH + 1):

            @pl.when(me + d < n)
            def _():
                out_b[step, part, d - 1] = packed_product(back_h[d - 1], back_l[d - 1], both_half[...])
                b_copy(step, part, d).start()

        acc[part] = packed_product(fwd_h[0], fwd_l[0], both_half[...])

    def one_turn(turn, carry):
        step, part = turn // 2, turn % 2
        for d in range(1, REACH + 1):

            @pl.when(me + d < n)
            def _():
                x_copy(step, part, d).wait_recv()
                put_stacked(both_half, 0, in_x[step, part, d - 1])
                acc[part] += packed_product(fwd_h[d], fwd_l[d], both_half[...])

        add_back(step, part)
        later = (step > 0).astype(F32)
        change = ((1.0 + later) * (1.0 / half_width)) * (acc[part] - center_shift * xs[step, part])
        xs[step + 1, part] = change - later * xs[jnp.maximum(step - 1, 0), part]

        @pl.when(turn < 4)
        def _():
            start_step(step + 1, part)

        if with_gram:

            @pl.when(turn >= 4)
            def _():
                f_copy(1, part).start()
                f_copy(0, part).start()

        return carry

    lax.fori_loop(0, 6, one_turn, 0)
    f_ref[:half], f_ref[half:] = unpacked(xs[3, 0], xs[3, 1])

    if with_gram:
        left_h, left_l = back_h.at[0, :width], back_l.at[0, :width]
        left_h[...], left_l[...] = halves(f_ref[...].T)
        total = rows * n
        owners, first_owner = n // 2, n // 4
        owner = jnp.clip(me - first_owner, 0, owners - 1)
        owns = (me >= first_owner) & (me < first_owner + owners)
        sizes = [width // owners, width // n] * 2
        mid = width // 2

        def rows_of(stage):
            return pl.ds(sum(sizes[:stage]), sizes[stage])

        def r_copy(stage, target, source):
            return pltpu.make_async_remote_copy(
                src_ref=parts.at[target, rows_of(stage)],
                dst_ref=in_r.at[source, rows_of(stage)],
                send_sem=rs_sem.at[stage, target],
                recv_sem=rr_sem.at[stage, source],
                device_id={"domain": first_owner + target},
            )

        def g_copy(stage, source, d):
            return pltpu.make_async_remote_copy(
                src_ref=in_g.at[source, rows_of(stage)],
                dst_ref=in_g.at[source, rows_of(stage)],
                send_sem=gs_sem.at[stage, d],
                recv_sem=gr_sem.at[stage, source],
                device_id={"domain": (me + d) % n},
            )

        def scatter(stage, block):
            parts[:, rows_of(stage)] = (block / total).reshape(owners, sizes[stage], width)
            for turn in range(owners):
                target = (me + turn) % owners

                @pl.when(me != first_owner + target)
                def _():
                    r_copy(stage, target, me).start()

        def multiply(stage, top, first, second):
            put_stacked(both, 0, first)
            put_stacked(both, 1, second)
            wide = jnp.dot(left_h[top:], both[...], preferred_element_type=F32)
            wide = wide + jnp.dot(left_l[top:], both[...], preferred_element_type=F32)
            first, second = wide[:, :width], wide[:, width:]
            first, second = first + swapped(first), second + swapped(second)
            scatter(stage, jnp.where(left_lanes(first), first, second))

        def add_up(stage):
            @pl.when(owns)
            def _():
                block = parts[owner, rows_of(stage)]
                for d in range(1, n):
                    source = (me + d) % n
                    r_copy(stage, owner, source).wait_recv()
                    block = block + in_r[source, rows_of(stage)]
                in_g[owner, rows_of(stage)] = block
                for d in range(1, n):
                    g_copy(stage, owner, d).start()

        def collected(stage):
            for source in range(owners):

                @pl.when(me != first_owner + source)
                def _():
                    g_copy(stage, source, 1).wait_recv()

            return in_g[:, rows_of(stage)].reshape(owners * sizes[stage], width)

        def columns_of(source):
            return pl.ds(pl.multiple_of(source * width, width), width)

        def t_copy(index):
            return pltpu.make_async_remote_copy(
                src_ref=out_t.at[index // 2],
                dst_ref=in_t.at[index],
                send_sem=ts_sem.at[index],
                recv_sem=tr_sem.at[index],
                device_id={"vec": (far, cross, near)[index]},
            )

        def turned(value):
            return jnp.concatenate([value, value], 0).T

        def put_upper(block, one, first, other, second):
            upper = block[:mid]
            left = left_lanes(upper)
            g_ref[:mid, columns_of(one)] = jnp.where(left, upper, first[:mid])
            g_ref[:mid, columns_of(other)] = jnp.where(left, swapped(upper), second[mid:])

        def put_lower(block, last, one, other):
            lower = block[mid:]
            left = left_lanes(lower)
            g_ref[mid:, columns_of(one)] = jnp.where(left, lower, swapped(last))
            g_ref[mid:, columns_of(other)] = jnp.where(left, swapped(lower), last)

        f_copy(0, 0).wait_recv()
        f_copy(2, 0).start()
        f_copy(2, 0).wait_recv()
        multiply(2, 0, in_f[0, 0], in_f[2, 0])
        f_copy(1, 0).wait_recv()
        multiply(0, 0, xs[3, 0], in_f[1, 0])
        f_copy(1, 1).wait_recv()
        multiply(1, mid, xs[3, 1], in_f[1, 1])
        f_copy(0, 1).wait_recv()
        f_copy(2, 1).start()
        f_copy(2, 1).wait_recv()
        multiply(3, mid, in_f[0, 1], in_f[2, 1])
        for stage in (2, 0, 1, 3):
            add_up(stage)
        block = collected(2)
        out_t[0] = block[mid:]
        t_copy(0).start()
        t_copy(1).start()
        mine_block = collected(0)
        out_t[1] = mine_block[mid:]
        t_copy(2).start()
        mine_turned = turned(mine_block[mid:])
        put_lower(mine_block, collected(1), mine, near)
        t_copy(2).wait_recv()
        put_upper(mine_block, mine, mine_turned, near, turned(in_t[2]))
        t_copy(0).wait_recv()
        t_copy(1).wait_recv()
        put_upper(block, far, turned(in_t[0]), cross, turned(in_t[1]))
        put_lower(block, collected(3), far, cross)
        for index in range(3):
            t_copy(index).wait_send()
        for index in range(3):
            for part in range(2):
                f_copy(index, part).wait_send()
        for stage in range(4):
            for target in range(owners):

                @pl.when(me != first_owner + target)
                def _():
                    r_copy(stage, target, me).wait_send()

        @pl.when(owns)
        def _():
            for stage in range(4):
                for d in range(1, n):
                    g_copy(stage, owner, d).wait_send()

    for d in range(1, REACH + 1):

        @pl.when(me >= d)
        def _():
            for step in range(3):
                for part in range(2):
                    x_copy(step, part, d).wait_send()

        @pl.when(me + d < n)
        def _():
            for step in range(3):
                for part in range(2):
                    b_copy(step, part, d).wait_send()


def shards(vectors, hamiltonian, tile_pairs, tile_counts):
    n = lax.axis_size("domain")
    m = lax.axis_size("vec")
    rows, width = vectors.shape
    groups = rows // TILE
    half = rows // 2
    slots = tile_pairs.shape[0]
    lanes = -(-max(slots, (REACH + 1) * groups * groups) // 128) * 128
    with_gram = m == 4 and n % 4 == 0 and width % (8 * n) == 0
    dma = pltpu.SemaphoreType.DMA
    out_shape = [jax.ShapeDtypeStruct((rows, width), F32)]
    scratch = [
        pltpu.VMEM(hamiltonian.shape, F32),
        pltpu.VMEM((rows, width), F32),
        pltpu.VMEM((2, slots), jnp.int32),
        pltpu.VMEM((2, lanes), jnp.int32),
        pltpu.SMEM((2, lanes), jnp.int32),
        pltpu.VMEM((REACH + 1, rows, rows), BF16),
        pltpu.VMEM((REACH + 1, rows, rows), BF16),
        pltpu.VMEM((REACH, rows, rows), BF16),
        pltpu.VMEM((REACH, rows, rows), BF16),
        pltpu.VMEM((rows, 2 * width), BF16),
        pltpu.VMEM((rows, width), BF16),
        pltpu.VMEM((2, half, width), F32),
        pltpu.VMEM((4, 2, half, width), F32),
        pltpu.VMEM((3, 2, REACH, half, width), F32),
        pltpu.VMEM((3, 2, REACH, half, width), F32),
        pltpu.VMEM((3, 2, REACH, half, width), F32),
        dma((4,)),
        dma((3, 2, REACH)),
        dma((3, 2, REACH)),
        dma((3, 2, REACH)),
        dma((3, 2, REACH)),
    ]
    if with_gram:
        out_shape.append(jax.ShapeDtypeStruct((width, m * width), F32))
        scratch += [
            pltpu.VMEM((3, 2, half, width), F32),
            pltpu.VMEM((n // 2, 6 * width // n, width), F32),
            pltpu.VMEM((n, 6 * width // n, width), F32),
            pltpu.VMEM((n // 2, 6 * width // n, width), F32),
            pltpu.VMEM((2, width // 2, width), F32),
            pltpu.VMEM((3, width // 2, width), F32),
            dma((3, 2)),
            dma((3, 2)),
            dma((4, n // 2)),
            dma((4, n)),
            dma((4, n)),
            dma((4, n // 2)),
            dma((3,)),
            dma((3,)),
        ]
    outs = pl.pallas_call(
        functools.partial(filter_kernel, n, m, with_gram),
        out_shape=out_shape,
        in_specs=[
            pl.BlockSpec(memory_space=pltpu.HBM),
            pl.BlockSpec(memory_space=pltpu.HBM),
            pl.BlockSpec(memory_space=pltpu.SMEM),
            pl.BlockSpec(memory_space=pltpu.HBM),
        ],
        out_specs=[pl.BlockSpec(memory_space=pltpu.VMEM)] * len(out_shape),
        scratch_shapes=scratch,
        compiler_params=pltpu.CompilerParams(
            collective_id=0, has_side_effects=True, vmem_limit_bytes=52 * 2**20
        ),
        name="chebyshev",
    )(pltpu.with_memory_space_constraint(vectors, pltpu.HBM), pltpu.with_memory_space_constraint(tile_pairs.T, pltpu.HBM), tile_counts, hamiltonian)
    if with_gram:
        return tuple(outs)
    (filtered,) = outs
    gathered = lax.all_gather(filtered, "vec", axis=1, tiled=True)
    partial_block = jnp.dot(
        filtered.T, gathered, precision=lax.Precision.HIGHEST, preferred_element_type=F32
    ) / (rows * n)
    return (filtered, lax.psum(partial_block, "domain"))


def solution(mesh):
    in_specs = (P("domain", "vec"), P("domain", None, None), P("domain", None), P("domain"))
    out_specs = (P("domain", "vec"), P("vec", None))
    return jax.shard_map(shards, mesh=mesh, in_specs=in_specs, out_specs=out_specs, check_vma=False)
```
